128 devices in a mesh: head: 2 (over core), seq: 64 (over x, z, y).
Axes of the slice: x: 4, y: 4, z: 4, core: 2. Of those that a mesh axis runs over, the one named last changes fastest.
Arguments:
- queries: bfloat16 [32768, 5120], P(('seq', 'head')), may hold values from -8 to 8
- key_states: bfloat16 [32768, 5120], P(('seq', 'head')), may hold values from -8 to 8
- value_states: bfloat16 [32768, 5120], P(('seq', 'head')), may hold values from -6 to 6
- cluster_perm: int32 [40, 32768], P('head', 'seq'), may hold values from 0 to 32767, as said below
- block_mask: int32 [40, 256, 256], P('head', 'seq'), may hold values from 0 to 1, as said below
Outputs:
- attention_out: bfloat16 [32768, 5120], P(('seq', 'head'))
The draws below stay inside these ranges and needn't reach their ends.
Inputs may be any that keep to these rules, and one draw needn't show every extreme that they name: `cluster_perm`: for each head, positions k * 512 to (k + 1) * 512 - 1 list the tokens k * 512 to (k + 1) * 512 - 1, each once. `block_mask`: for each head and each aligned run of 4 query blocks, the key blocks used by some query block of the run number exactly 4. For such a run and the 20 heads g * 20 to (g + 1) * 20 - 1, the (head, key block) pairs so used that lie in one aligned run of 4 key blocks number at most 2, and exactly 2 in some run. Every query block uses 1 to 4 key blocks, and some query block of every run uses 4, for every head.
All inputs are finite; a program needn't handle non-finite values.
Results may differ from the reference program's by a relative error of at most 0.0049.
Values may be sent and summed in bfloat16 or wider, within the bound.
No kernel may reach another device: no remote copies, remote signals or barrier semaphores. Data moves between devices by JAX's collectives and lax.ppermute only.
A program may use at most 128 MiB of HBM per device.

```python
import math
import jax
import jax.numpy as jnp
from jax import lax

HEADS = 40
HEAD_DIM = 128
BLOCK = 128
ROWS_SEQ = 512
TOKENS = 32768
BLOCKS = 256
PICKS = 4
LIVE = 4
CAP = 2
N_HEAD = 2
N_SEQ = 64


def draw_queries(key, part):
    gaussian = jax.random.truncated_normal(jax.random.fold_in(key, 11), -6.0, 6.0, (TOKENS, HEADS, HEAD_DIM), jnp.float32)
    return gaussian.reshape(TOKENS, HEADS * HEAD_DIM).astype(jnp.bfloat16)


def draw_key_states(key, part):
    gaussian = jax.random.truncated_normal(jax.random.fold_in(key, 21), -6.0, 6.0, (TOKENS, HEADS, HEAD_DIM), jnp.float32)
    return gaussian.reshape(TOKENS, HEADS * HEAD_DIM).astype(jnp.bfloat16)


def draw_cluster_perm(key, part):
    random_bits = jax.random.bits(jax.random.fold_in(key, 31), (HEADS, N_SEQ, ROWS_SEQ))
    local_order = jnp.argsort(random_bits, axis=-1, stable=True).astype(jnp.int32)
    offsets = (jnp.arange(N_SEQ, dtype=jnp.int32) * ROWS_SEQ)[None, :, None]
    return (local_order + offsets).reshape(HEADS, TOKENS)


def draw_block_mask(key, part):
    heads_group = HEADS // N_HEAD
    shard_blocks = ROWS_SEQ // BLOCK
    slot_count = N_SEQ * CAP
    filled_count = heads_group * PICKS
    slot_owner = jnp.arange(slot_count, dtype=jnp.int32) // CAP
    slot_index = jnp.arange(slot_count, dtype=jnp.int32) % CAP
    star_owner = jax.random.randint(jax.random.fold_in(key, 41), (N_HEAD, N_SEQ), 0, N_SEQ)
    jitter = jax.random.randint(jax.random.fold_in(key, 42), (N_HEAD, N_SEQ, slot_count), 0, 1 << 20)
    priority = jitter + jnp.where(slot_owner[None, None, :] == star_owner[:, :, None], 0, 1 << 21)
    ranking = jnp.argsort(priority, axis=-1, stable=True)
    position = jnp.argsort(ranking, axis=-1, stable=True).astype(jnp.int32)
    is_filled = (position < filled_count).astype(jnp.int32)
    head_local = position % heads_group
    rotate = jax.random.randint(jax.random.fold_in(key, 43), (N_HEAD, N_SEQ, N_SEQ * heads_group), 0, shard_blocks)
    rot_pick = jnp.take_along_axis(rotate, slot_owner[None, None, :] * heads_group + head_local, axis=-1)
    key_block = slot_owner[None, None, :] * shard_blocks + (slot_index[None, None, :] + rot_pick) % shard_blocks
    group_ids = jnp.arange(N_HEAD, dtype=jnp.int32)[:, None, None]
    shard_ids = jnp.arange(N_SEQ, dtype=jnp.int32)[None, :, None]
    needed = jnp.zeros((N_HEAD, N_SEQ, heads_group, BLOCKS), jnp.int32)
    needed = needed.at[group_ids, shard_ids, head_local, key_block].max(is_filled)
    prefix = (jnp.cumsum(needed, axis=-1) - needed).astype(jnp.int32)
    chosen = (needed[..., None] == 1) & (prefix[..., None] == jnp.arange(PICKS, dtype=jnp.int32))
    picked = jnp.sum(jnp.where(chosen, jnp.arange(BLOCKS, dtype=jnp.int32)[:, None], 0), axis=-2).astype(jnp.int32)
    pick_ids = jnp.arange(PICKS, dtype=jnp.int32)
    query_ids = jnp.arange(shard_blocks, dtype=jnp.int32)
    home_bits = pick_ids[None, :] % shard_blocks == query_ids[:, None]
    home_count = jnp.sum(home_bits, axis=1).astype(jnp.int32)
    target = jax.random.randint(jax.random.fold_in(key, 44), (N_HEAD, N_SEQ, heads_group, shard_blocks), 1, LIVE + 1)
    star_query = jax.random.randint(jax.random.fold_in(key, 45), (N_HEAD, N_SEQ, heads_group), 0, shard_blocks)
    target = jnp.where(query_ids == star_query[..., None], LIVE, target)
    target = jnp.maximum(target, home_count)
    draw_scores = jax.random.randint(jax.random.fold_in(key, 46), (N_HEAD, N_SEQ, heads_group, shard_blocks, PICKS), 0, 1 << 20)
    draw_scores = jnp.where(home_bits, 1 << 21, draw_scores)
    extra_rank = jnp.argsort(jnp.argsort(draw_scores, axis=-1, stable=True), axis=-1, stable=True).astype(jnp.int32)
    live_bits = (home_bits | (extra_rank < (target - home_count)[..., None])).astype(jnp.int32)
    mask_grid = jnp.zeros((N_HEAD, N_SEQ, heads_group, shard_blocks, BLOCKS), jnp.int32)
    mask_grid = mask_grid.at[jnp.arange(N_HEAD)[:, None, None, None, None], jnp.arange(N_SEQ)[None, :, None, None, None], jnp.arange(heads_group)[None, None, :, None, None], query_ids[None, None, None, :, None], picked[:, :, :, None, :]].max(live_bits)
    return mask_grid.transpose(0, 2, 1, 3, 4).reshape(HEADS, BLOCKS, BLOCKS)


def level_of(stream_key, shape, cuts, low, high):
    def one(dim, shards_of):
        draws = jax.random.uniform(jax.random.fold_in(jax.random.fold_in(stream_key, 6), dim), (shards_of,), jnp.float32, low / len(cuts), high / len(cuts))
        return jnp.repeat(jnp.exp(draws), shape[dim] // shards_of).reshape((-1,) + (1,) * (len(shape) - dim - 1))

    gain = one(*cuts[0])
    for cut in cuts[1:]:
        gain = gain * one(*cut)
    return gain


def scatter_about(stream_key, shape, deviation, bound, split=(), kind=jnp.bfloat16):
    gain = level_of(stream_key, shape, split, -0.22, 0.18) if split else 1.0
    array = jax.random.normal(stream_key, shape, jnp.float32) * deviation * gain
    return jnp.minimum(jnp.maximum(array, -bound), bound).astype(kind)


def setup_inputs(seed: int = 0) -> dict:
    seeds = jax.random.split(jax.random.key(seed), 6)
    return {
        "queries": draw_queries(jax.random.fold_in(seeds[5], 71), 0),
        "key_states": draw_key_states(jax.random.fold_in(seeds[5], 71), 0),
        "value_states": scatter_about(seeds[2], (TOKENS, HEADS * HEAD_DIM), 1.0, 6.0, ((0, 128),)),
        "cluster_perm": draw_cluster_perm(jax.random.fold_in(seeds[5], 71), 0),
        "block_mask": draw_block_mask(jax.random.fold_in(seeds[5], 71), 0),
    }


def reference(queries, key_states, value_states, cluster_perm, block_mask):

    def cluster_order(flat_rows):
        grid_view = flat_rows.reshape(TOKENS, HEADS, HEAD_DIM).transpose(1, 0, 2)
        return jnp.take_along_axis(grid_view, cluster_perm[:, :, None].astype(jnp.int32), axis=1)
    query_sorted = cluster_order(queries)
    key_sorted = cluster_order(key_states)
    value_sorted = cluster_order(value_states)
    score_scale = 1.0 / math.sqrt(HEAD_DIM)
    slot_ids = jnp.arange(LIVE, dtype=jnp.int32)
    block_ids = jnp.arange(BLOCKS, dtype=jnp.int32)

    def one_head(operands):
        query_head, key_head, value_head, mask_head = operands
        prefix = (jnp.cumsum(mask_head, axis=1) - mask_head).astype(jnp.int32)
        chosen = (mask_head[:, :, None] == 1) & (prefix[:, :, None] == slot_ids[None, None, :])
        which_block = lax.optimization_barrier(jnp.sum(jnp.where(chosen, block_ids[None, :, None], 0), axis=1)).astype(jnp.int32)
        usable = jnp.any(chosen, axis=1)
        key_sel = jnp.take(key_head.reshape(BLOCKS, BLOCK, HEAD_DIM), which_block, axis=0)
        value_sel = jnp.take(value_head.reshape(BLOCKS, BLOCK, HEAD_DIM), which_block, axis=0)
        query_blocks = query_head.reshape(BLOCKS, BLOCK, HEAD_DIM).astype(jnp.float32)
        scores = jnp.einsum('nid,nljd->nilj', query_blocks, key_sel.astype(jnp.float32), precision=lax.Precision.HIGHEST) * score_scale
        scores = jnp.where(usable[:, None, :, None], scores, -jnp.inf)
        row_top = lax.optimization_barrier(jnp.max(scores, axis=(2, 3), keepdims=True))
        exponent = jnp.exp(scores - row_top)
        row_total = lax.optimization_barrier(jnp.sum(exponent, axis=(2, 3), keepdims=True))
        weights = (exponent / row_total).astype(jnp.bfloat16)
        attended = jnp.einsum('nilj,nljd->nid', weights.astype(jnp.float32), value_sel.astype(jnp.float32), precision=lax.Precision.HIGHEST)
        return attended.astype(jnp.bfloat16).reshape(TOKENS, HEAD_DIM)
    attended = lax.map(one_head, (query_sorted, key_sorted, value_sorted, block_mask))
    restored = jnp.zeros((HEADS, TOKENS, HEAD_DIM), jnp.bfloat16)
    restored = restored.at[jnp.arange(HEADS, dtype=jnp.int32)[:, None], cluster_perm.astype(jnp.int32)].set(attended)
    return restored.transpose(1, 0, 2).reshape(TOKENS, HEADS * HEAD_DIM)
```

```python
import functools
import math

import jax
import jax.numpy as jnp
from jax import lax
from jax.experimental import pallas as pl
from jax.experimental.pallas import tpu as pltpu
from jax.sharding import PartitionSpec as P

HEAD_DIM = 128
BLOCK = 128
CAPACITY = 2
PICKS = 4
HEADS_STEP = 4
MASKED = -1e30


def request_kernel(mask_ref, table_ref):
    heads, shard_blocks, blocks = mask_ref.shape
    shards = table_ref.shape[0]
    mask = mask_ref[...]
    needed = jnp.max(mask, axis=1)
    key_block = lax.broadcasted_iota(jnp.int32, (heads, blocks), 1)
    head = lax.broadcasted_iota(jnp.int32, (heads, blocks), 0)
    pair = head * shard_blocks + lax.rem(key_block, shard_blocks)
    low = jnp.min(jnp.where(needed > 0, pair, heads * shard_blocks), axis=0, keepdims=True)
    high = jnp.max(jnp.where(needed > 0, pair, -1), axis=0, keepdims=True)
    owner = lax.broadcasted_iota(jnp.int32, (shards, blocks), 1) // shard_blocks
    mine = owner == lax.broadcasted_iota(jnp.int32, (shards, blocks), 0)
    low_col = jnp.min(jnp.where(mine, low, heads * shard_blocks), axis=1, keepdims=True)
    high_col = jnp.max(jnp.where(mine, high, -1), axis=1, keepdims=True)
    low_col = jnp.minimum(low_col, heads * shard_blocks - 1)
    high_col = jnp.maximum(high_col, 0)
    lane = lax.broadcasted_iota(jnp.int32, (shards, 128), 1)
    table_ref[...] = jnp.where(lane == 0, low_col, high_col)


def plan_kernel(mask_ref, position_ref, bias_ref):
    heads, shard_blocks, blocks = mask_ref.shape
    shards = blocks // shard_blocks
    mask = mask_ref[...]
    needed = jnp.max(mask, axis=1)
    key_block = lax.broadcasted_iota(jnp.int32, (heads, blocks), 1)
    head = lax.broadcasted_iota(jnp.int32, (heads, blocks), 0)
    pair = head * shard_blocks + lax.rem(key_block, shard_blocks)
    low = jnp.min(jnp.where(needed > 0, pair, heads * shard_blocks), axis=0, keepdims=True)
    owner = lax.broadcasted_iota(jnp.int32, (shards, blocks), 1) // shard_blocks
    mine = owner == lax.broadcasted_iota(jnp.int32, (shards, blocks), 0)
    low_col = jnp.min(jnp.where(mine, low, heads * shard_blocks), axis=1, keepdims=True)
    low_own = jnp.min(jnp.where(mine, low_col, heads * shard_blocks), axis=0, keepdims=True)
    slot = (key_block // shard_blocks) * CAPACITY + (pair != low_own).astype(jnp.int32)
    upper = (
        lax.broadcasted_iota(jnp.int32, (blocks, blocks), 0)
        < lax.broadcasted_iota(jnp.int32, (blocks, blocks), 1)
    )
    prefix = jnp.dot(
        needed.astype(jnp.float32).astype(jnp.bfloat16),
        jnp.where(upper, 1.0, 0.0).astype(jnp.bfloat16),
        preferred_element_type=jnp.float32,
    )
    lane = lax.broadcasted_iota(jnp.int32, (heads, 128), 1)
    row = lax.broadcasted_iota(jnp.int32, (heads, 128), 0)
    position = jnp.zeros((heads, 128), jnp.int32)
    for j in range(PICKS):
        chosen = (needed > 0) & (prefix == float(j))
        slot_j = jnp.sum(jnp.where(chosen, slot, 0), axis=1, keepdims=True)
        position = jnp.where(lane == j, slot_j, position)
        bias = jnp.zeros((heads, 128), jnp.float32)
        for q in range(shard_blocks):
            live = jnp.max(jnp.where(chosen, mask[:, q, :], 0), axis=1, keepdims=True)
            bias = jnp.where(
                (lane == row * shard_blocks + q) & (live == 0), MASKED, bias
            )
        bias_ref[j] = bias
    position_ref[...] = position


def sort_kernel(meta, column_ref, key_own, key_far, value_own, value_far, key_out, value_out):
    del meta
    rows = column_ref.shape[1]
    half = rows // 2
    token = lax.broadcasted_iota(jnp.int32, (rows, rows), 1)
    for k in range(HEADS_STEP):
        cut = slice(k * HEAD_DIM, (k + 1) * HEAD_DIM)
        order = jnp.where(column_ref[0, :, k : k + 1] == token, 1.0, 0.0).astype(jnp.bfloat16)
        own = jnp.concatenate([key_own[:, cut], value_own[:, cut]], axis=1)
        far = jnp.concatenate([key_far[:, cut], value_far[:, cut]], axis=1)
        both = jnp.concatenate([own, far], axis=0)
        ordered = jnp.dot(order, both, preferred_element_type=jnp.float32).astype(jnp.bfloat16)
        key_out[k] = ordered[:, :HEAD_DIM]
        value_out[k] = ordered[:, HEAD_DIM:]


def scatter_kernel(request_ref, blocks_ref, send_ref, sem):
    shards = request_ref.shape[0]

    def start(d, carry):
        for j in range(CAPACITY):
            pltpu.make_async_copy(
                blocks_ref.at[request_ref[d, j]], send_ref.at[d * CAPACITY + j], sem
            ).start()
        return carry

    lax.fori_loop(0, shards, start, 0)
    pltpu.make_async_copy(send_ref, send_ref, sem).wait()


def member_kernel(perm_ref, member_ref):
    heads, rows = perm_ref.shape
    shard_blocks = rows // BLOCK
    token = lax.broadcasted_iota(jnp.int32, (rows, rows), 0)
    block = lax.broadcasted_iota(jnp.int32, (rows, 128), 0) // BLOCK
    lane = lax.broadcasted_iota(jnp.int32, (rows, 128), 1)

    def step(h, total):
        place = jnp.where(perm_ref[pl.ds(h, 1), :] == token, 1.0, 0.0).astype(jnp.bfloat16)
        target = jnp.where(lane == h * shard_blocks + block, 1.0, 0.0).astype(jnp.bfloat16)
        return total + jnp.dot(place, target, preferred_element_type=jnp.float32)

    total = lax.fori_loop(0, heads, step, jnp.zeros((rows, 128), jnp.float32))
    member_ref[...] = total.astype(jnp.bfloat16)


def score_kernel(meta, position, *refs):
    del meta, position
    query_own, query_far, member_ref, bias_ref = refs[:4]
    keys = refs[4 : 4 + PICKS]
    weight_ref = refs[4 + PICKS]
    h = pl.program_id(0)
    query = jnp.concatenate([query_own[...], query_far[...]], axis=0)
    left = jnp.concatenate([query, member_ref[...]], axis=1)
    right = []
    for j in range(PICKS):
        bias = bias_ref[j, pl.ds(h, 1), :].astype(jnp.bfloat16)
        right.append(
            jnp.concatenate([keys[j][0], jnp.broadcast_to(bias, (BLOCK, 128))], axis=1)
        )
    right = jnp.concatenate(right, axis=0)
    scores = lax.dot_general(
        left, right, (((1,), (1,)), ((), ())), preferred_element_type=jnp.float32
    )
    top = jnp.max(scores, axis=1, keepdims=True)
    exponent = jnp.exp2((scores - top) * (math.log2(math.e) / math.sqrt(HEAD_DIM)))
    total = jnp.sum(exponent, axis=1, keepdims=True)
    weight_ref[0] = (exponent * (1.0 / total)).astype(jnp.bfloat16)


def mix_kernel(meta, position, *refs):
    del meta, position
    weight_ref, out_ref = refs[0], refs[-1]
    values = refs[1:-1]
    for k in range(HEADS_STEP):
        value = jnp.concatenate([values[k * PICKS + j][0] for j in range(PICKS)], axis=0)
        mixed = jnp.dot(weight_ref[k], value, preferred_element_type=jnp.float32)
        out_ref[:, k * HEAD_DIM : (k + 1) * HEAD_DIM] = mixed.astype(jnp.bfloat16)


def place_kernel(meta, out_in, far_ref, out_ref, sem):
    del out_in
    width = far_ref.shape[1]
    start = pl.multiple_of((1 - meta[0]) * width, 128)
    copy = pltpu.make_async_copy(far_ref, out_ref.at[:, pl.ds(start, width)], sem)
    copy.start()
    copy.wait()


def shards(queries, key_states, value_states, cluster_perm, block_mask):
    heads, rows = cluster_perm.shape
    half, columns = queries.shape
    width = heads * HEAD_DIM
    shard_blocks = rows // BLOCK
    seq_count = lax.axis_size("seq")
    pairs = heads * shard_blocks
    slots = seq_count * CAPACITY
    steps = heads // HEADS_STEP
    step_width = HEADS_STEP * HEAD_DIM
    core = lax.axis_index("head")
    meta = jnp.stack([core, lax.axis_index("seq")]).astype(jnp.int32)
    vmem = pl.BlockSpec(memory_space=pltpu.VMEM)
    smem = pl.BlockSpec(memory_space=pltpu.SMEM)
    hbm = pl.BlockSpec(memory_space=pl.ANY)
    big = pltpu.CompilerParams(vmem_limit_bytes=56 << 20)

    table = pl.pallas_call(
        request_kernel,
        out_shape=jax.ShapeDtypeStruct((seq_count, 128), jnp.int32),
        in_specs=[vmem],
        out_specs=vmem,
        name="request",
    )(block_mask)
    requested = lax.all_to_all(
        table.reshape(seq_count, 1, 128), "seq", split_axis=0, concat_axis=0, tiled=True
    ).reshape(seq_count, 128)

    def swap(x):
        return lax.ppermute(x, "head", [(0, 1), (1, 0)])

    def far_half(x):
        return swap(lax.dynamic_slice(x, (0, (1 - core) * width), (half, width)))

    key_far = far_half(key_states)
    value_far = far_half(value_states)
    query_far = far_half(queries)

    local_perm = jnp.bitwise_and(
        cluster_perm - lax.axis_index("seq") * rows + core * half, rows - 1
    )
    column = local_perm.reshape(steps, HEADS_STEP, rows).transpose(0, 2, 1)

    own_spec = pl.BlockSpec((half, step_width), lambda g, meta: (0, meta[0] * steps + g))
    far_spec = pl.BlockSpec((half, step_width), lambda g, meta: (0, g))
    sorted_spec = pl.BlockSpec((HEADS_STEP, rows, HEAD_DIM), lambda g, meta: (g, 0, 0))
    key_sorted, value_sorted = pl.pallas_call(
        sort_kernel,
        out_shape=[jax.ShapeDtypeStruct((heads, rows, HEAD_DIM), jnp.bfloat16)] * 2,
        grid_spec=pltpu.PrefetchScalarGridSpec(
            num_scalar_prefetch=1,
            grid=(steps,),
            in_specs=[
                pl.BlockSpec((1, rows, HEADS_STEP), lambda g, meta: (g, 0, 0)),
                own_spec,
                far_spec,
                own_spec,
                far_spec,
            ],
            out_specs=[sorted_spec] * 2,
        ),
        compiler_params=big,
        name="sort",
    )(meta, column, key_states, key_far, value_states, value_far)

    def exchange(blocks):
        send = pl.pallas_call(
            scatter_kernel,
            out_shape=jax.ShapeDtypeStruct((slots, BLOCK, HEAD_DIM), jnp.bfloat16),
            in_specs=[smem, hbm],
            out_specs=hbm,
            scratch_shapes=[pltpu.SemaphoreType.DMA],
            name="scatter",
        )(requested, blocks.reshape(pairs, BLOCK, HEAD_DIM))
        return lax.all_to_all(send, "seq", split_axis=0, concat_axis=0, tiled=True)

    key_got = exchange(key_sorted)
    value_got = exchange(value_sorted)

    member = pl.pallas_call(
        member_kernel,
        out_shape=jax.ShapeDtypeStruct((rows, 128), jnp.bfloat16),
        in_specs=[vmem],
        out_specs=vmem,
        compiler_params=big,
        name="member",
    )(local_perm)
    position, bias = pl.pallas_call(
        plan_kernel,
        out_shape=[
            jax.ShapeDtypeStruct((heads, 128), jnp.int32),
            jax.ShapeDtypeStruct((PICKS, heads, 128), jnp.float32),
        ],
        in_specs=[vmem],
        out_specs=[vmem] * 2,
        name="plan",
    )(block_mask)

    def pick_spec(heads_step, k, j):
        return pl.BlockSpec(
            (1, BLOCK, HEAD_DIM),
            lambda g, meta, position: (position[g * heads_step + k, j], 0, 0),
        )

    weights = pl.pallas_call(
        score_kernel,
        out_shape=jax.ShapeDtypeStruct((heads, rows, PICKS * BLOCK), jnp.bfloat16),
        grid_spec=pltpu.PrefetchScalarGridSpec(
            num_scalar_prefetch=2,
            grid=(heads,),
            in_specs=[
                pl.BlockSpec((half, HEAD_DIM), lambda h, meta, position: (0, meta[0] * heads + h)),
                pl.BlockSpec((half, HEAD_DIM), lambda h, meta, position: (0, h)),
                pl.BlockSpec((rows, 128), lambda h, meta, position: (0, 0)),
                pl.BlockSpec((PICKS, heads, 128), lambda h, meta, position: (0, 0, 0)),
            ]
            + [pick_spec(1, 0, j) for j in range(PICKS)],
            out_specs=pl.BlockSpec(
                (1, rows, PICKS * BLOCK), lambda h, meta, position: (h, 0, 0)
            ),
        ),
        compiler_params=big,
        name="score",
    )(meta, position, queries, query_far, member, bias, *([key_got] * PICKS))

    def mix(part, out_columns, column_map):
        return pl.pallas_call(
            mix_kernel,
            out_shape=jax.ShapeDtypeStruct((half, out_columns), jnp.bfloat16),
            grid_spec=pltpu.PrefetchScalarGridSpec(
                num_scalar_prefetch=2,
                grid=(steps,),
                in_specs=[
                    pl.BlockSpec(
                        (HEADS_STEP, half, PICKS * BLOCK),
                        lambda g, meta, position: (g, part, 0),
                    )
                ]
                + [
                    pick_spec(HEADS_STEP, k, j)
                    for k in range(HEADS_STEP)
                    for j in range(PICKS)
                ],
                out_specs=pl.BlockSpec((half, step_width), column_map),
            ),
            compiler_params=big,
            name="mix",
        )(meta, position, weights, *([value_got] * (HEADS_STEP * PICKS)))

    out_far = swap(mix(1, width, lambda g, meta, position: (0, g)))
    out_own = mix(0, columns, lambda g, meta, position: (0, meta[0] * steps + g))
    return pl.pallas_call(
        place_kernel,
        out_shape=jax.ShapeDtypeStruct((half, columns), jnp.bfloat16),
        in_specs=[smem, hbm, hbm],
        out_specs=hbm,
        scratch_shapes=[pltpu.SemaphoreType.DMA],
        input_output_aliases={1: 0},
        name="place",
    )(meta, out_own, out_far)


def solution(mesh):
    placed = (
        P(("seq", "head"), None),
        P(("seq", "head"), None),
        P(("seq", "head"), None),
        P("head", "seq"),
        P("head", "seq", None),
    )
    return jax.shard_map(
        shards, mesh=mesh, in_specs=placed, out_specs=P(("seq", "head"), None), check_vma=False
    )
```

```python
import functools
import math

import jax
import jax.numpy as jnp
from jax import lax
from jax.experimental import pallas as pl
from jax.experimental.pallas import tpu as pltpu
from jax.sharding import PartitionSpec as P

HEAD_DIM = 128
BLOCK = 128
CAPACITY = 2
PICKS = 4
HEADS_STEP = 4
MASKED = -1e30


def request_kernel(mask_ref, table_ref):
    heads, shard_blocks, blocks = mask_ref.shape
    shards = table_ref.shape[0]
    mask = mask_ref[...]
    needed = jnp.max(mask, axis=1)
    key_block = lax.broadcasted_iota(jnp.int32, (heads, blocks), 1)
    head = lax.broadcasted_iota(jnp.int32, (heads, blocks), 0)
    pair = head * shard_blocks + lax.rem(key_block, shard_blocks)
    low = jnp.min(jnp.where(needed > 0, pair, heads * shard_blocks), axis=0, keepdims=True)
    high = jnp.max(jnp.where(needed > 0, pair, -1), axis=0, keepdims=True)
    owner = lax.broadcasted_iota(jnp.int32, (shards, blocks), 1) // shard_blocks
    mine = owner == lax.broadcasted_iota(jnp.int32, (shards, blocks), 0)
    low_col = jnp.min(jnp.where(mine, low, heads * shard_blocks), axis=1, keepdims=True)
    high_col = jnp.max(jnp.where(mine, high, -1), axis=1, keepdims=True)
    low_col = jnp.minimum(low_col, heads * shard_blocks - 1)
    high_col = jnp.maximum(high_col, 0)
    lane = lax.broadcasted_iota(jnp.int32, (shards, 128), 1)
    table_ref[...] = jnp.where(lane == 0, low_col, high_col)


def plan_kernel(mask_ref, position_ref, bias_ref):
    heads, shard_blocks, blocks = mask_ref.shape
    shards = blocks // shard_blocks
    mask = mask_ref[...]
    needed = jnp.max(mask, axis=1)
    key_block = lax.broadcasted_iota(jnp.int32, (heads, blocks), 1)
    head = lax.broadcasted_iota(jnp.int32, (heads, blocks), 0)
    pair = head * shard_blocks + lax.rem(key_block, shard_blocks)
    low = jnp.min(jnp.where(needed > 0, pair, heads * shard_blocks), axis=0, keepdims=True)
    owner = lax.broadcasted_iota(jnp.int32, (shards, blocks), 1) // shard_blocks
    mine = owner == lax.broadcasted_iota(jnp.int32, (shards, blocks), 0)
    low_col = jnp.min(jnp.where(mine, low, heads * shard_blocks), axis=1, keepdims=True)
    low_own = jnp.min(jnp.where(mine, low_col, heads * shard_blocks), axis=0, keepdims=True)
    slot = (key_block // shard_blocks) * CAPACITY + (pair != low_own).astype(jnp.int32)
    upper = (
        lax.broadcasted_iota(jnp.int32, (blocks, blocks), 0)
        < lax.broadcasted_iota(jnp.int32, (blocks, blocks), 1)
    )
    prefix = jnp.dot(
        needed.astype(jnp.float32).astype(jnp.bfloat16),
        jnp.where(upper, 1.0, 0.0).astype(jnp.bfloat16),
        preferred_element_type=jnp.float32,
    )
    lane = lax.broadcasted_iota(jnp.int32, (heads, 128), 1)
    row = lax.broadcasted_iota(jnp.int32, (heads, 128), 0)
    position = jnp.zeros((heads, 128), jnp.int32)
    for j in range(PICKS):
        chosen = (needed > 0) & (prefix == float(j))
        slot_j = jnp.sum(jnp.where(chosen, slot, 0), axis=1, keepdims=True)
        position = jnp.where(lane == j, slot_j, position)
        bias = jnp.zeros((heads, 128), jnp.float32)
        for q in range(shard_blocks):
            live = jnp.max(jnp.where(chosen, mask[:, q, :], 0), axis=1, keepdims=True)
            bias = jnp.where(
                (lane == row * shard_blocks + q) & (live == 0), MASKED, bias
            )
        bias_ref[j] = bias
    position_ref[...] = position


def sort_kernel(meta, column_ref, key_own, key_far, value_own, value_far, key_out, value_out):
    del meta
    rows = column_ref.shape[1]
    half = rows // 2
    token = lax.broadcasted_iota(jnp.int32, (rows, rows), 1)
    for k in range(HEADS_STEP):
        cut = slice(k * HEAD_DIM, (k + 1) * HEAD_DIM)
        order = jnp.where(column_ref[0, :, k : k + 1] == token, 1.0, 0.0).astype(jnp.bfloat16)
        own = jnp.concatenate([key_own[:, cut], value_own[:, cut]], axis=1)
        far = jnp.concatenate([key_far[:, cut], value_far[:, cut]], axis=1)
        both = jnp.concatenate([own, far], axis=0)
        ordered = jnp.dot(order, both, preferred_element_type=jnp.float32).astype(jnp.bfloat16)
        key_out[k] = ordered[:, :HEAD_DIM]
        value_out[k] = ordered[:, HEAD_DIM:]


def scatter_kernel(request_ref, blocks_ref, send_ref, sem):
    shards = request_ref.shape[0]

    def start(d, carry):
        for j in range(CAPACITY):
            pltpu.make_async_copy(
                blocks_ref.at[request_ref[d, j]], send_ref.at[d * CAPACITY + j], sem
            ).start()
        return carry

    lax.fori_loop(0, shards, start, 0)
    pltpu.make_async_copy(send_ref, send_ref, sem).wait()


def member_kernel(perm_ref, member_ref):
    heads, rows = perm_ref.shape
    shard_blocks = rows // BLOCK
    token = lax.broadcasted_iota(jnp.int32, (rows, rows), 0)
    block = lax.broadcasted_iota(jnp.int32, (rows, 128), 0) // BLOCK
    lane = lax.broadcasted_iota(jnp.int32, (rows, 128), 1)

    def step(h, total):
        place = jnp.where(perm_ref[pl.ds(h, 1), :] == token, 1.0, 0.0).astype(jnp.bfloat16)
        target = jnp.where(lane == h * shard_blocks + block, 1.0, 0.0).astype(jnp.bfloat16)
        return total + jnp.dot(place, target, preferred_element_type=jnp.float32)

    total = lax.fori_loop(0, heads, step, jnp.zeros((rows, 128), jnp.float32))
    member_ref[...] = total.astype(jnp.bfloat16)


def score_kernel(meta, position, *refs):
    del meta, position
    query_own, query_far, member_ref, bias_ref = refs[:4]
    keys = refs[4 : 4 + PICKS]
    weight_ref = refs[4 + PICKS]
    h = pl.program_id(0)
    query = jnp.concatenate([query_own[...], query_far[...]], axis=0)
    left = jnp.concatenate([query, member_ref[...]], axis=1)
    right = []
    for j in range(PICKS):
        bias = bias_ref[j, pl.ds(h, 1), :].astype(jnp.bfloat16)
        right.append(
            jnp.concatenate([keys[j][0], jnp.broadcast_to(bias, (BLOCK, 128))], axis=1)
        )
    right = jnp.concatenate(right, axis=0)
    scores = lax.dot_general(
        left, right, (((1,), (1,)), ((), ())), preferred_element_type=jnp.float32
    )
    top = jnp.max(scores, axis=1, keepdims=True)
    exponent = jnp.exp2((scores - top) * (math.log2(math.e) / math.sqrt(HEAD_DIM)))
    total = jnp.sum(exponent, axis=1, keepdims=True)
    weight_ref[0] = (exponent * (1.0 / total)).astype(jnp.bfloat16)


def mix_kernel(meta, position, *refs):
    del meta, position
    weight_ref, out_ref = refs[0], refs[-1]
    values = refs[1:-1]
    for k in range(HEADS_STEP):
        value = jnp.concatenate([values[k * PICKS + j][0] for j in range(PICKS)], axis=0)
        mixed = jnp.dot(weight_ref[k], value, preferred_element_type=jnp.float32)
        out_ref[:, k * HEAD_DIM : (k + 1) * HEAD_DIM] = mixed.astype(jnp.bfloat16)


def place_kernel(meta, out_in, far_ref, out_ref, sem):
    del out_in
    width = far_ref.shape[1]
    start = pl.multiple_of((1 - meta[0]) * width, 128)
    copy = pltpu.make_async_copy(far_ref, out_ref.at[:, pl.ds(start, width)], sem)
    copy.start()
    copy.wait()


def shards(queries, key_states, value_states, cluster_perm, block_mask):
    heads, rows = cluster_perm.shape
    half, columns = queries.shape
    width = heads * HEAD_DIM
    shard_blocks = rows // BLOCK
    seq_count = lax.axis_size("seq")
    pairs = heads * shard_blocks
    slots = seq_count * CAPACITY
    steps = heads // HEADS_STEP
    step_width = HEADS_STEP * HEAD_DIM
    core = lax.axis_index("head")
    meta = jnp.stack([core, lax.axis_index("seq")]).astype(jnp.int32)
    vmem = pl.BlockSpec(memory_space=pltpu.VMEM)
    smem = pl.BlockSpec(memory_space=pltpu.SMEM)
    hbm = pl.BlockSpec(memory_space=pl.ANY)
    big = pltpu.CompilerParams(vmem_limit_bytes=56 << 20)

    table = pl.pallas_call(
        request_kernel,
        out_shape=jax.ShapeDtypeStruct((seq_count, 128), jnp.int32),
        in_specs=[vmem],
        out_specs=vmem,
        name="request",
    )(block_mask)
    requested = lax.all_to_all(
        table.reshape(seq_count, 1, 128), "seq", split_axis=0, concat_axis=0, tiled=True
    ).reshape(seq_count, 128)

    def swap(x):
        return lax.ppermute(x, "head", [(0, 1), (1, 0)])

    def far_half(x):
        return swap(lax.dynamic_slice(x, (0, (1 - core) * width), (half, width)))

    key_far = far_half(key_states)
    value_far = far_half(value_states)
    query_far = far_half(queries)

    local_perm = jnp.bitwise_and(
        cluster_perm - lax.axis_index("seq") * rows + core * half, rows - 1
    )
    column = local_perm.reshape(steps, HEADS_STEP, rows).transpose(0, 2, 1)

    own_spec = pl.BlockSpec((half, step_width), lambda g, meta: (0, meta[0] * steps + g))
    far_spec = pl.BlockSpec((half, step_width), lambda g, meta: (0, g))
    sorted_spec = pl.BlockSpec((HEADS_STEP, rows, HEAD_DIM), lambda g, meta: (g, 0, 0))
    key_sorted, value_sorted = pl.pallas_call(
        sort_kernel,
        out_shape=[jax.ShapeDtypeStruct((heads, rows, HEAD_DIM), jnp.bfloat16)] * 2,
        grid_spec=pltpu.PrefetchScalarGridSpec(
            num_scalar_prefetch=1,
            grid=(steps,),
            in_specs=[
                pl.BlockSpec((1, rows, HEADS_STEP), lambda g, meta: (g, 0, 0)),
                own_spec,
                far_spec,
                own_spec,
                far_spec,
            ],
            out_specs=[sorted_spec] * 2,
        ),
        compiler_params=big,
        name="sort",
    )(meta, column, key_states, key_far, value_states, value_far)

    def exchange(blocks):
        send = pl.pallas_call(
            scatter_kernel,
            out_shape=jax.ShapeDtypeStruct((slots, BLOCK, HEAD_DIM), jnp.bfloat16),
            in_specs=[smem, vmem],
            out_specs=hbm,
            scratch_shapes=[pltpu.SemaphoreType.DMA],
            compiler_params=pltpu.CompilerParams(vmem_limit_bytes=16 << 20),
            name="scatter",
        )(requested, blocks.reshape(pairs, BLOCK, HEAD_DIM))
        return lax.all_to_all(send, "seq", split_axis=0, concat_axis=0, tiled=True)

    key_got = exchange(key_sorted)
    value_got = exchange(value_sorted)

    member = pl.pallas_call(
        member_kernel,
        out_shape=jax.ShapeDtypeStruct((rows, 128), jnp.bfloat16),
        in_specs=[vmem],
        out_specs=vmem,
        compiler_params=big,
        name="member",
    )(local_perm)
    position, bias = pl.pallas_call(
        plan_kernel,
        out_shape=[
            jax.ShapeDtypeStruct((heads, 128), jnp.int32),
            jax.ShapeDtypeStruct((PICKS, heads, 128), jnp.float32),
        ],
        in_specs=[vmem],
        out_specs=[vmem] * 2,
        name="plan",
    )(block_mask)

    def pick_spec(heads_step, k, j):
        return pl.BlockSpec(
            (1, BLOCK, HEAD_DIM),
            lambda g, meta, position: (position[g * heads_step + k, j], 0, 0),
        )

    weights = pl.pallas_call(
        score_kernel,
        out_shape=jax.ShapeDtypeStruct((heads, rows, PICKS * BLOCK), jnp.bfloat16),
        grid_spec=pltpu.PrefetchScalarGridSpec(
            num_scalar_prefetch=2,
            grid=(heads,),
            in_specs=[
                pl.BlockSpec((half, HEAD_DIM), lambda h, meta, position: (0, meta[0] * heads + h)),
                pl.BlockSpec((half, HEAD_DIM), lambda h, meta, position: (0, h)),
                pl.BlockSpec((rows, 128), lambda h, meta, position: (0, 0)),
                pl.BlockSpec((PICKS, heads, 128), lambda h, meta, position: (0, 0, 0)),
            ]
            + [pick_spec(1, 0, j) for j in range(PICKS)],
            out_specs=pl.BlockSpec(
                (1, rows, PICKS * BLOCK), lambda h, meta, position: (h, 0, 0)
            ),
        ),
        compiler_params=big,
        name="score",
    )(meta, position, queries, query_far, member, bias, *([key_got] * PICKS))

    def mix(part, out_columns, column_map):
        return pl.pallas_call(
            mix_kernel,
            out_shape=jax.ShapeDtypeStruct((half, out_columns), jnp.bfloat16),
            grid_spec=pltpu.PrefetchScalarGridSpec(
                num_scalar_prefetch=2,
                grid=(steps,),
                in_specs=[
                    pl.BlockSpec(
                        (HEADS_STEP, half, PICKS * BLOCK),
                        lambda g, meta, position: (g, part, 0),
                    )
                ]
                + [
                    pick_spec(HEADS_STEP, k, j)
                    for k in range(HEADS_STEP)
                    for j in range(PICKS)
                ],
                out_specs=pl.BlockSpec((half, step_width), column_map),
            ),
            compiler_params=big,
            name="mix",
        )(meta, position, weights, *([value_got] * (HEADS_STEP * PICKS)))

    out_far = swap(mix(1, width, lambda g, meta, position: (0, g)))
    out_own = mix(0, columns, lambda g, meta, position: (0, meta[0] * steps + g))
    return pl.pallas_call(
        place_kernel,
        out_shape=jax.ShapeDtypeStruct((half, columns), jnp.bfloat16),
        in_specs=[smem, hbm, vmem],
        out_specs=hbm,
        scratch_shapes=[pltpu.SemaphoreType.DMA],
        input_output_aliases={1: 0},
        name="place",
    )(meta, out_own, out_far)


def solution(mesh):
    placed = (
        P(("seq", "head"), None),
        P(("seq", "head"), None),
        P(("seq", "head"), None),
        P("head", "seq"),
        P("head", "seq", None),
    )
    return jax.shard_map(
        shards, mesh=mesh, in_specs=placed, out_specs=P(("seq", "head"), None), check_vma=False
    )
```

```python
import math

import jax
import jax.numpy as jnp
from jax import lax
from jax.experimental import pallas as pl
from jax.experimental.pallas import tpu as pltpu
from jax.sharding import PartitionSpec as P

HEAD_DIM = 128
BLOCK = 128
CAPACITY = 2
PICKS = 4
HEADS_STEP = 4
MASKED = -1e30


def slot_lows(needed, shard_blocks):
    heads, blocks = needed.shape
    shards = blocks // shard_blocks
    key_block = lax.broadcasted_iota(jnp.int32, (heads, blocks), 1)
    head = lax.broadcasted_iota(jnp.int32, (heads, blocks), 0)
    pair = head * shard_blocks + lax.rem(key_block, shard_blocks)
    low = jnp.min(jnp.where(needed > 0, pair, heads * shard_blocks), axis=0, keepdims=True)
    owner = lax.broadcasted_iota(jnp.int32, (shards, blocks), 1) // shard_blocks
    mine = owner == lax.broadcasted_iota(jnp.int32, (shards, blocks), 0)
    low_col = jnp.min(jnp.where(mine, low, heads * shard_blocks), axis=1, keepdims=True)
    return pair, mine, low_col


def request_kernel(mask_ref, table_ref):
    heads, shard_blocks, _ = mask_ref.shape
    needed = jnp.max(mask_ref[...], axis=1)
    pair, mine, low_col = slot_lows(needed, shard_blocks)
    high = jnp.max(jnp.where(needed > 0, pair, -1), axis=0, keepdims=True)
    high_col = jnp.max(jnp.where(mine, high, -1), axis=1, keepdims=True)
    low_col = jnp.minimum(low_col, heads * shard_blocks - 1)
    high_col = jnp.maximum(high_col, 0)
    lane = lax.broadcasted_iota(jnp.int32, table_ref.shape, 1)
    table_ref[...] = jnp.where(lane == 0, low_col, high_col)


def local_tokens(perm, rows):
    return jnp.bitwise_and(perm + lax.axis_index("head") * (rows // 2), rows - 1)


def sort_kernel(perm_ref, key_own, key_far, value_own, value_far, out_ref, perm_pad, buf, sem):
    heads, rows = perm_ref.shape
    steps, _, half, step_width = buf.shape
    shard_blocks = rows // BLOCK
    base = lax.axis_index("head") * (heads * HEAD_DIM)

    def copies(g):
        cut = pl.ds(pl.multiple_of(base + g * step_width, 128), step_width)
        return [
            pltpu.make_async_copy(ref.at[:, cut], buf.at[g, n], sem.at[g, n])
            for n, ref in enumerate((key_own, value_own, key_far, value_far))
        ]

    for g in range(steps):
        for copy in copies(g):
            copy.start()
    perm_pad[0:heads, :] = local_tokens(perm_ref[...], rows)
    column = jnp.transpose(perm_pad[...])
    token = lax.broadcasted_iota(jnp.int32, (rows, rows), 1)
    for g in range(steps):
        for copy in copies(g):
            copy.wait()
        for k in range(HEADS_STEP):
            h = g * HEADS_STEP + k
            cut = slice(k * HEAD_DIM, (k + 1) * HEAD_DIM)
            order = jnp.where(column[:, h : h + 1] == token, 1.0, 0.0).astype(jnp.bfloat16)
            own = jnp.concatenate([buf[g, 0, :, cut], buf[g, 1, :, cut]], axis=1)
            far = jnp.concatenate([buf[g, 2, :, cut], buf[g, 3, :, cut]], axis=1)
            both = jnp.concatenate([own, far], axis=0)
            ordered = jnp.dot(order, both, preferred_element_type=jnp.float32)
            ordered = ordered.astype(jnp.bfloat16)
            for b in range(shard_blocks):
                block = ordered[b * BLOCK : (b + 1) * BLOCK]
                out_ref[h * shard_blocks + b, 0:BLOCK] = block[:, :HEAD_DIM]
                out_ref[h * shard_blocks + b, BLOCK : 2 * BLOCK] = block[:, HEAD_DIM:]


def scatter_kernel(request_ref, blocks_ref, send_ref, sem):
    shards = request_ref.shape[0]

    def start(d, carry):
        for j in range(CAPACITY):
            pltpu.make_async_copy(
                blocks_ref.at[request_ref[d, j]], send_ref.at[d * CAPACITY + j], sem
            ).start()
        return carry

    lax.fori_loop(0, shards, start, 0, unroll=4)
    pltpu.make_async_copy(send_ref, send_ref, sem).wait()


def prepare_kernel(
    perm_ref, mask_ref, query_own, query_far, query_ref, member_ref, position_ref, bias_ref, sem
):
    heads, rows = perm_ref.shape
    _, shard_blocks, blocks = mask_ref.shape
    half = rows // 2
    width = heads * HEAD_DIM
    cut = pl.ds(pl.multiple_of(lax.axis_index("head") * width, 128), width)
    copies = [
        pltpu.make_async_copy(query_own.at[:, cut], query_ref.at[0:half, :], sem.at[0]),
        pltpu.make_async_copy(query_far.at[:, cut], query_ref.at[half:rows, :], sem.at[1]),
    ]
    for copy in copies:
        copy.start()

    token = lax.broadcasted_iota(jnp.int32, (rows, rows), 0)
    block = lax.broadcasted_iota(jnp.int32, (rows, 128), 0) // BLOCK
    lane = lax.broadcasted_iota(jnp.int32, (rows, 128), 1)

    def step(h, total):
        local = local_tokens(perm_ref[pl.ds(h, 1), :], rows)
        place = jnp.where(local == token, 1.0, 0.0).astype(jnp.bfloat16)
        target = jnp.where(lane == h * shard_blocks + block, 1.0, 0.0).astype(jnp.bfloat16)
        return total + jnp.dot(place, target, preferred_element_type=jnp.float32)

    total = lax.fori_loop(0, heads, step, jnp.zeros((rows, 128), jnp.float32))
    member_ref[...] = total.astype(jnp.bfloat16)

    mask = mask_ref[...]
    needed = jnp.max(mask, axis=1)
    pair, mine, low_col = slot_lows(needed, shard_blocks)
    low_own = jnp.min(jnp.where(mine, low_col, heads * shard_blocks), axis=0, keepdims=True)
    key_block = lax.broadcasted_iota(jnp.int32, (heads, blocks), 1)
    slot = (key_block // shard_blocks) * CAPACITY + (pair != low_own).astype(jnp.int32)
    upper = (
        lax.broadcasted_iota(jnp.int32, (blocks, blocks), 0)
        < lax.broadcasted_iota(jnp.int32, (blocks, blocks), 1)
    )
    prefix = jnp.dot(
        needed.astype(jnp.float32).astype(jnp.bfloat16),
        jnp.where(upper, 1.0, 0.0).astype(jnp.bfloat16),
        preferred_element_type=jnp.float32,
    )
    lane = lax.broadcasted_iota(jnp.int32, (heads, 128), 1)
    row = lax.broadcasted_iota(jnp.int32, (heads, 128), 0)
    position = jnp.zeros((heads, 128), jnp.int32)
    for j in range(PICKS):
        chosen = (needed > 0) & (prefix == float(j))
        slot_j = jnp.sum(jnp.where(chosen, slot, 0), axis=1, keepdims=True)
        position = jnp.where(lane == j, slot_j, position)
        bias = jnp.zeros((heads, 128), jnp.float32)
        for q in range(shard_blocks):
            live = jnp.max(jnp.where(chosen, mask[:, q, :], 0), axis=1, keepdims=True)
            bias = jnp.where((lane == row * shard_blocks + q) & (live == 0), MASKED, bias)
        bias_ref[j] = bias
    position_ref[...] = position
    for copy in copies:
        copy.wait()


def attend(h, query, member, bias_ref, blocks_ref):
    left = jnp.concatenate([query, member], axis=1)
    keys, values = [], []
    for j in range(PICKS):
        bias = bias_ref[j, pl.ds(h, 1), :].astype(jnp.bfloat16)
        bias = jnp.broadcast_to(bias, (BLOCK, 128))
        keys.append(jnp.concatenate([blocks_ref[h * PICKS + j, 0:BLOCK], bias], axis=1))
        values.append(blocks_ref[h * PICKS + j, BLOCK : 2 * BLOCK])
    keys = jnp.concatenate(keys, axis=0)
    values = jnp.concatenate(values, axis=0)
    scores = lax.dot_general(
        left, keys, (((1,), (1,)), ((), ())), preferred_element_type=jnp.float32
    )
    top = jnp.max(scores, axis=1, keepdims=True)
    exponent = jnp.exp2((scores - top) * (math.log2(math.e) / math.sqrt(HEAD_DIM)))
    total = jnp.sum(exponent, axis=1, keepdims=True)
    weights = (exponent * (1.0 / total)).astype(jnp.bfloat16)
    return jnp.dot(weights, values, preferred_element_type=jnp.float32).astype(jnp.bfloat16)


def far_kernel(
    position_ref, query_ref, member_ref, bias_ref, got_ref, out_ref, blocks_ref, sem
):
    heads = position_ref.shape[0]
    half = out_ref.shape[0]

    def start(h, carry):
        for j in range(PICKS):
            pltpu.make_async_copy(
                got_ref.at[position_ref[h, j]], blocks_ref.at[h * PICKS + j], sem.at[h]
            ).start()
        return carry

    lax.fori_loop(0, heads, start, 0, unroll=2)
    for h in range(heads):
        part = blocks_ref.at[h * PICKS : (h + 1) * PICKS]
        pltpu.make_async_copy(part, part, sem.at[h]).wait()
        cut = slice(h * HEAD_DIM, (h + 1) * HEAD_DIM)
        out_ref[:, cut] = attend(
            h, query_ref[half:, cut], member_ref[half:, :], bias_ref, blocks_ref
        )


def own_kernel(query_ref, member_ref, bias_ref, blocks_ref, out_ref, stage, sem):
    half, width = stage.shape
    heads = width // HEAD_DIM
    step_width = HEADS_STEP * HEAD_DIM
    base = lax.axis_index("head") * width

    def copy(g):
        return pltpu.make_async_copy(
            stage.at[:, g * step_width : (g + 1) * step_width],
            out_ref.at[:, pl.ds(pl.multiple_of(base + g * step_width, 128), step_width)],
            sem.at[g],
        )

    for h in range(heads):
        cut = slice(h * HEAD_DIM, (h + 1) * HEAD_DIM)
        stage[:, cut] = attend(
            h, query_ref[:half, cut], member_ref[:half, :], bias_ref, blocks_ref
        )
        if h % HEADS_STEP == HEADS_STEP - 1:
            copy(h // HEADS_STEP).start()
    for g in range(heads // HEADS_STEP):
        copy(g).wait()


def place_kernel(out_in, far_ref, out_ref, sem):
    del out_in
    width = far_ref.shape[1]
    start = pl.multiple_of((1 - lax.axis_index("head")) * width, 128)
    copy = pltpu.make_async_copy(far_ref, out_ref.at[:, pl.ds(start, width)], sem)
    copy.start()
    copy.wait()


def shards(queries, key_states, value_states, cluster_perm, block_mask):
    heads, rows = cluster_perm.shape
    half, columns = queries.shape
    width = heads * HEAD_DIM
    shard_blocks = rows // BLOCK
    seq_count = lax.axis_size("seq")
    pairs = heads * shard_blocks
    slots = seq_count * CAPACITY
    steps = heads // HEADS_STEP
    vmem = pl.BlockSpec(memory_space=pltpu.VMEM)
    smem = pl.BlockSpec(memory_space=pltpu.SMEM)
    hbm = pl.BlockSpec(memory_space=pltpu.HBM)
    limit = lambda mib: pltpu.CompilerParams(vmem_limit_bytes=mib << 20)
    held = lambda x: pltpu.with_memory_space_constraint(x, pltpu.VMEM)
    held_out = lambda shape, dtype: pltpu.VMEM(shape, dtype)
    hbm_out = lambda shape, dtype: pltpu.HBM(shape, dtype)
    dma = pltpu.SemaphoreType.DMA
    bf16 = jnp.bfloat16

    table = pl.pallas_call(
        request_kernel,
        out_shape=jax.ShapeDtypeStruct((seq_count, 128), jnp.int32),
        in_specs=[vmem],
        out_specs=vmem,
        name="request",
    )(block_mask)
    requested = lax.all_to_all(
        table.reshape(seq_count, 1, 128), "seq", split_axis=0, concat_axis=0, tiled=True
    ).reshape(seq_count, 128)

    def swap(x):
        return lax.ppermute(x, "head", [(0, 1), (1, 0)])

    key_far = swap(key_states)
    value_far = swap(value_states)

    blocks = pl.pallas_call(
        sort_kernel,
        out_shape=held_out((pairs, 2 * BLOCK, HEAD_DIM), bf16),
        in_specs=[vmem, hbm, hbm, hbm, hbm],
        out_specs=vmem,
        scratch_shapes=[
            pltpu.VMEM((128, rows), jnp.int32),
            pltpu.VMEM((steps, 4, half, HEADS_STEP * HEAD_DIM), bf16),
            dma((steps, 4)),
        ],
        compiler_params=limit(24),
        name="sort",
    )(cluster_perm, key_states, key_far, value_states, value_far)
    send = pl.pallas_call(
        scatter_kernel,
        out_shape=hbm_out((slots, 2 * BLOCK, HEAD_DIM), bf16),
        in_specs=[smem, vmem],
        out_specs=hbm,
        scratch_shapes=[dma],
        compiler_params=limit(16),
        name="scatter",
    )(requested, held(blocks))
    got = lax.all_to_all(send, "seq", split_axis=0, concat_axis=0, tiled=True)

    query, member, position, bias = pl.pallas_call(
        prepare_kernel,
        out_shape=[
            held_out((rows, width), bf16),
            jax.ShapeDtypeStruct((rows, 128), bf16),
            jax.ShapeDtypeStruct((heads, 128), jnp.int32),
            jax.ShapeDtypeStruct((PICKS, heads, 128), jnp.float32),
        ],
        in_specs=[vmem, vmem, hbm, hbm],
        out_specs=[vmem] * 4,
        scratch_shapes=[dma((2,))],
        compiler_params=limit(24),
        name="prepare",
    )(cluster_perm, block_mask, queries, swap(queries))

    out_far, picked = pl.pallas_call(
        far_kernel,
        out_shape=[
            jax.ShapeDtypeStruct((half, width), bf16),
            held_out((pairs, 2 * BLOCK, HEAD_DIM), bf16),
        ],
        in_specs=[smem, vmem, vmem, vmem, hbm],
        out_specs=[vmem, vmem],
        scratch_shapes=[dma((heads,))],
        compiler_params=limit(32),
        name="far_rows",
    )(position, held(query), member, bias, got)
    out_far = swap(out_far)
    out_own = pl.pallas_call(
        own_kernel,
        out_shape=hbm_out((half, columns), bf16),
        in_specs=[vmem] * 4,
        out_specs=hbm,
        scratch_shapes=[pltpu.VMEM((half, width), bf16), dma((steps,))],
        compiler_params=limit(32),
        name="own_rows",
    )(held(query), member, bias, held(picked))
    return pl.pallas_call(
        place_kernel,
        out_shape=hbm_out((half, columns), bf16),
        in_specs=[hbm, vmem],
        out_specs=hbm,
        scratch_shapes=[dma],
        input_output_aliases={0: 0},
        name="place",
    )(out_own, held(out_far))


def solution(mesh):
    placed = (
        P(("seq", "head"), None),
        P(("seq", "head"), None),
        P(("seq", "head"), None),
        P("head", "seq"),
        P("head", "seq", None),
    )
    return jax.shard_map(
        shards, mesh=mesh, in_specs=placed, out_specs=P(("seq", "head"), None), check_vma=False
    )
```

```python
import math

import jax
import jax.numpy as jnp
from jax import lax
from jax.experimental import pallas as pl
from jax.experimental.pallas import tpu as pltpu
from jax.sharding import PartitionSpec as P

HEAD_DIM = 128
BLOCK = 128
CAPACITY = 2
PICKS = 4
HEADS_STEP = 4
MASKED = -1e30


def slot_lows(needed, shard_blocks):
    heads, blocks = needed.shape
    shards = blocks // shard_blocks
    key_block = lax.broadcasted_iota(jnp.int32, (heads, blocks), 1)
    head = lax.broadcasted_iota(jnp.int32, (heads, blocks), 0)
    pair = head * shard_blocks + lax.rem(key_block, shard_blocks)
    low = jnp.min(jnp.where(needed > 0, pair, heads * shard_blocks), axis=0, keepdims=True)
    owner = lax.broadcasted_iota(jnp.int32, (shards, blocks), 1) // shard_blocks
    mine = owner == lax.broadcasted_iota(jnp.int32, (shards, blocks), 0)
    low_col = jnp.min(jnp.where(mine, low, heads * shard_blocks), axis=1, keepdims=True)
    return pair, mine, low_col


def request_kernel(mask_ref, table_ref):
    heads, shard_blocks, _ = mask_ref.shape
    needed = jnp.max(mask_ref[...], axis=1)
    pair, mine, low_col = slot_lows(needed, shard_blocks)
    high = jnp.max(jnp.where(needed > 0, pair, -1), axis=0, keepdims=True)
    high_col = jnp.max(jnp.where(mine, high, -1), axis=1, keepdims=True)
    low_col = jnp.minimum(low_col, heads * shard_blocks - 1)
    high_col = jnp.maximum(high_col, 0)
    lane = lax.broadcasted_iota(jnp.int32, table_ref.shape, 1)
    table_ref[...] = jnp.where(lane == 0, low_col, high_col)


def local_tokens(perm, rows):
    return jnp.bitwise_and(perm + lax.axis_index("head") * (rows // 2), rows - 1)


def plan_kernel(mask_ref, position_ref, bias_ref):
    heads, shard_blocks, blocks = mask_ref.shape
    mask = mask_ref[...]
    needed = jnp.max(mask, axis=1)
    pair, mine, low_col = slot_lows(needed, shard_blocks)
    low_own = jnp.min(jnp.where(mine, low_col, heads * shard_blocks), axis=0, keepdims=True)
    key_block = lax.broadcasted_iota(jnp.int32, (heads, blocks), 1)
    slot = (key_block // shard_blocks) * CAPACITY + (pair != low_own).astype(jnp.int32)
    upper = (
        lax.broadcasted_iota(jnp.int32, (blocks, blocks), 0)
        < lax.broadcasted_iota(jnp.int32, (blocks, blocks), 1)
    )
    prefix = jnp.dot(
        needed.astype(jnp.float32).astype(jnp.bfloat16),
        jnp.where(upper, 1.0, 0.0).astype(jnp.bfloat16),
        preferred_element_type=jnp.float32,
    )
    lane = lax.broadcasted_iota(jnp.int32, (heads, 128), 1)
    row = lax.broadcasted_iota(jnp.int32, (heads, 128), 0)
    position = jnp.zeros((heads, 128), jnp.int32)
    for j in range(PICKS):
        chosen = (needed > 0) & (prefix == float(j))
        slot_j = jnp.sum(jnp.where(chosen, slot, 0), axis=1, keepdims=True)
        position = jnp.where(lane == j, slot_j, position)
        bias = jnp.zeros((heads, 128), jnp.float32)
        for q in range(shard_blocks):
            live = jnp.max(jnp.where(chosen, mask[:, q, :], 0), axis=1, keepdims=True)
            bias = jnp.where((lane == row * shard_blocks + q) & (live == 0), MASKED, bias)
        bias_ref[j] = bias
    position_ref[...] = position


def sort_kernel(
    request_ref, perm_ref, key_own, key_far, value_own, value_far,
    send_ref, member_ref, perm_pad, member_pad, buf, out_ref, sem, send_sem,
):
    heads, rows = perm_ref.shape
    steps, _, half, step_width = buf.shape
    shard_blocks = rows // BLOCK
    base = lax.axis_index("head") * (heads * HEAD_DIM)

    def copies(g):
        cut = pl.ds(pl.multiple_of(base + g * step_width, 128), step_width)
        return [
            pltpu.make_async_copy(ref.at[:, cut], buf.at[g, n], sem.at[g, n])
            for n, ref in enumerate((key_own, value_own, key_far, value_far))
        ]

    for g in range(steps):
        for copy in copies(g):
            copy.start()
    perm_pad[0:heads, :] = local_tokens(perm_ref[...], rows)
    column = jnp.transpose(perm_pad[...])
    token = lax.broadcasted_iota(jnp.int32, (rows, rows), 1)
    member_pad[heads * shard_blocks :, :] = jnp.zeros(
        (member_pad.shape[0] - heads * shard_blocks, rows), jnp.float32
    )
    for g in range(steps):
        for copy in copies(g):
            copy.wait()
        for k in range(HEADS_STEP):
            h = g * HEADS_STEP + k
            cut = slice(k * HEAD_DIM, (k + 1) * HEAD_DIM)
            order = jnp.where(column[:, h : h + 1] == token, 1.0, 0.0)
            own = jnp.concatenate([buf[g, 0, :, cut], buf[g, 1, :, cut]], axis=1)
            far = jnp.concatenate([buf[g, 2, :, cut], buf[g, 3, :, cut]], axis=1)
            both = jnp.concatenate([own, far], axis=0)
            ordered = jnp.dot(
                order.astype(jnp.bfloat16), both, preferred_element_type=jnp.float32
            ).astype(jnp.bfloat16)
            for b in range(shard_blocks):
                part = slice(b * BLOCK, (b + 1) * BLOCK)
                row = h * shard_blocks + b
                member_pad[row : row + 1, :] = jnp.sum(order[part], axis=0, keepdims=True)
                out_ref[row, 0:BLOCK] = ordered[part, :HEAD_DIM]
                out_ref[row, BLOCK : 2 * BLOCK] = ordered[part, HEAD_DIM:]

    def start(d, carry):
        for j in range(CAPACITY):
            pltpu.make_async_copy(
                out_ref.at[request_ref[d, j]], send_ref.at[d * CAPACITY + j], send_sem
            ).start()
        return carry

    lax.fori_loop(0, request_ref.shape[0], start, 0, unroll=8)
    member_ref[...] = jnp.transpose(member_pad[...]).astype(jnp.bfloat16)
    pltpu.make_async_copy(send_ref, send_ref, send_sem).wait()


def score(h, query, member, bias_ref, blocks_ref):
    left = jnp.concatenate([query, member], axis=1)
    keys = []
    for j in range(PICKS):
        bias = jnp.broadcast_to(bias_ref[j, h : h + 1, :].astype(jnp.bfloat16), (BLOCK, 128))
        keys.append(jnp.concatenate([blocks_ref[h * PICKS + j, 0:BLOCK], bias], axis=1))
    return lax.dot_general(
        left,
        jnp.concatenate(keys, axis=0),
        (((1,), (1,)), ((), ())),
        preferred_element_type=jnp.float32,
    )


def mix(h, scores, blocks_ref):
    top = jnp.max(scores, axis=1, keepdims=True)
    exponent = jnp.exp2((scores - top) * (math.log2(math.e) / math.sqrt(HEAD_DIM)))
    total = jnp.sum(exponent, axis=1, keepdims=True)
    weights = (exponent * (1.0 / total)).astype(jnp.bfloat16)
    values = jnp.concatenate(
        [blocks_ref[h * PICKS + j, BLOCK : 2 * BLOCK] for j in range(PICKS)], axis=0
    )
    return jnp.dot(weights, values, preferred_element_type=jnp.float32).astype(jnp.bfloat16)


def attend(heads, ready, query_ref, member, bias_ref, blocks_ref, finish):
    def score_of(h):
        ready(h)
        cut = slice(h * HEAD_DIM, (h + 1) * HEAD_DIM)
        return score(h, query_ref[:, cut], member, bias_ref, blocks_ref)

    following = score_of(0)
    for h in range(heads):
        scores = following
        if h + 1 < heads:
            following = score_of(h + 1)
        finish(h, mix(h, scores, blocks_ref))


def query_copy(query_hbm, query_ref, sem):
    width = query_ref.shape[1]
    cut = pl.ds(pl.multiple_of(lax.axis_index("head") * width, 128), width)
    return pltpu.make_async_copy(query_hbm.at[:, cut], query_ref, sem)


def far_kernel(
    position_ref, member_ref, bias_ref, query_hbm, got_ref, out_ref, blocks_ref, query_ref, sem
):
    heads = position_ref.shape[0]
    half = out_ref.shape[0]
    load = query_copy(query_hbm, query_ref, sem.at[heads])
    load.start()

    def start(h, carry):
        for j in range(PICKS):
            pltpu.make_async_copy(
                got_ref.at[position_ref[h, j]], blocks_ref.at[h * PICKS + j], sem.at[h]
            ).start()
        return carry

    lax.fori_loop(0, heads, start, 0, unroll=4)
    load.wait()

    def ready(h):
        part = blocks_ref.at[h * PICKS : (h + 1) * PICKS]
        pltpu.make_async_copy(part, part, sem.at[h]).wait()

    def finish(h, mixed):
        out_ref[:, h * HEAD_DIM : (h + 1) * HEAD_DIM] = mixed

    attend(heads, ready, query_ref, member_ref[half:, :], bias_ref, blocks_ref, finish)


def own_kernel(
    member_ref, bias_ref, blocks_ref, query_hbm, out_ref, query_ref, stage, sem, query_sem
):
    half, width = stage.shape
    heads = width // HEAD_DIM
    step_width = HEADS_STEP * HEAD_DIM
    base = lax.axis_index("head") * width
    load = query_copy(query_hbm, query_ref, query_sem)
    load.start()

    def copy(g):
        return pltpu.make_async_copy(
            stage.at[:, g * step_width : (g + 1) * step_width],
            out_ref.at[:, pl.ds(pl.multiple_of(base + g * step_width, 128), step_width)],
            sem.at[g],
        )

    def finish(h, mixed):
        stage[:, h * HEAD_DIM : (h + 1) * HEAD_DIM] = mixed
        if h % HEADS_STEP == HEADS_STEP - 1:
            copy(h // HEADS_STEP).start()

    load.wait()
    attend(
        heads, lambda h: None, query_ref, member_ref[:half, :], bias_ref, blocks_ref, finish
    )
    for g in range(heads // HEADS_STEP):
        copy(g).wait()


def place_kernel(out_in, far_ref, out_ref, sem):
    del out_in
    width = far_ref.shape[1]
    start = pl.multiple_of((1 - lax.axis_index("head")) * width, 128)
    copy = pltpu.make_async_copy(far_ref, out_ref.at[:, pl.ds(start, width)], sem)
    copy.start()
    copy.wait()


def shards(queries, key_states, value_states, cluster_perm, block_mask):
    heads, rows = cluster_perm.shape
    half, columns = queries.shape
    width = heads * HEAD_DIM
    shard_blocks = rows // BLOCK
    seq_count = lax.axis_size("seq")
    pairs = heads * shard_blocks
    slots = seq_count * CAPACITY
    steps = heads // HEADS_STEP
    vmem = pl.BlockSpec(memory_space=pltpu.VMEM)
    smem = pl.BlockSpec(memory_space=pltpu.SMEM)
    hbm = pl.BlockSpec(memory_space=pltpu.HBM)
    limit = lambda mib: pltpu.CompilerParams(vmem_limit_bytes=mib << 20)
    held = lambda x: pltpu.with_memory_space_constraint(x, pltpu.VMEM)
    far = lambda x: pltpu.with_memory_space_constraint(x, pltpu.HBM)
    held_out = lambda shape, dtype: pltpu.VMEM(shape, dtype)
    hbm_out = lambda shape, dtype: pltpu.HBM(shape, dtype)
    dma = pltpu.SemaphoreType.DMA
    bf16 = jnp.bfloat16

    table = pl.pallas_call(
        request_kernel,
        out_shape=jax.ShapeDtypeStruct((seq_count, 128), jnp.int32),
        in_specs=[vmem],
        out_specs=vmem,
        name="request",
    )(block_mask)
    requested = lax.all_to_all(
        table.reshape(seq_count, 1, 128), "seq", split_axis=0, concat_axis=0, tiled=True
    ).reshape(seq_count, 128)

    def swap(x):
        return lax.ppermute(x, "head", [(0, 1), (1, 0)])

    key_far = swap(key_states)
    value_far = swap(value_states)

    query_far = swap(queries)
    position, bias = pl.pallas_call(
        plan_kernel,
        out_shape=[
            jax.ShapeDtypeStruct((heads, 128), jnp.int32),
            jax.ShapeDtypeStruct((PICKS, heads, 128), jnp.float32),
        ],
        in_specs=[vmem],
        out_specs=[vmem] * 2,
        name="plan",
    )(block_mask)
    send, member = pl.pallas_call(
        sort_kernel,
        out_shape=[
            hbm_out((slots, 2 * BLOCK, HEAD_DIM), bf16),
            held_out((rows, 128), bf16),
        ],
        in_specs=[smem, vmem, hbm, hbm, hbm, hbm],
        out_specs=[hbm, vmem],
        scratch_shapes=[
            pltpu.VMEM((128, rows), jnp.int32),
            pltpu.VMEM((128, rows), jnp.float32),
            pltpu.VMEM((steps, 4, half, HEADS_STEP * HEAD_DIM), bf16),
            pltpu.VMEM((pairs, 2 * BLOCK, HEAD_DIM), bf16),
            dma((steps, 4)),
            dma,
        ],
        compiler_params=limit(32),
        name="sort",
    )(requested, cluster_perm, far(key_states), key_far, far(value_states), value_far)
    send, member, position, bias, query_far = lax.optimization_barrier(
        (send, member, position, bias, query_far)
    )
    got = lax.all_to_all(send, "seq", split_axis=0, concat_axis=0, tiled=True)

    out_far, picked = pl.pallas_call(
        far_kernel,
        out_shape=[
            held_out((half, width), bf16),
            held_out((pairs, 2 * BLOCK, HEAD_DIM), bf16),
        ],
        in_specs=[smem, vmem, vmem, hbm, hbm],
        out_specs=[vmem, vmem],
        scratch_shapes=[pltpu.VMEM((half, width), bf16), dma((heads + 1,))],
        compiler_params=limit(32),
        name="far_rows",
    )(position, held(member), bias, query_far, far(got))
    out_far = swap(out_far)
    out_own = pl.pallas_call(
        own_kernel,
        out_shape=hbm_out((half, columns), bf16),
        in_specs=[vmem, vmem, vmem, hbm],
        out_specs=hbm,
        scratch_shapes=[
            pltpu.VMEM((half, width), bf16),
            pltpu.VMEM((half, width), bf16),
            dma((steps,)),
            dma,
        ],
        compiler_params=limit(32),
        name="own_rows",
    )(held(member), bias, held(picked), far(queries))
    return pl.pallas_call(
        place_kernel,
        out_shape=hbm_out((half, columns), bf16),
        in_specs=[hbm, vmem],
        out_specs=hbm,
        scratch_shapes=[dma],
        input_output_aliases={0: 0},
        name="place",
    )(out_own, held(out_far))


def solution(mesh):
    placed = (
        P(("seq", "head"), None),
        P(("seq", "head"), None),
        P(("seq", "head"), None),
        P("head", "seq"),
        P("head", "seq", None),
    )
    return jax.shard_map(
        shards, mesh=mesh, in_specs=placed, out_specs=P(("seq", "head"), None), check_vma=False
    )
```

```python
import math

import jax
import jax.numpy as jnp
from jax import lax
from jax.experimental import pallas as pl
from jax.experimental.pallas import tpu as pltpu
from jax.sharding import PartitionSpec as P

HEAD_DIM = 128
BLOCK = 128
CAPACITY = 2
PICKS = 4
HEADS_STEP = 4
SORT_STEP = 10
GATHERS = 1
MASKED = -1e30


def shift_of(count):
    return count.bit_length() - 1


def slot_lows(needed, shard_blocks):
    heads, blocks = needed.shape
    shards = blocks // shard_blocks
    key_block = lax.broadcasted_iota(jnp.int32, (heads, blocks), 1)
    head = lax.broadcasted_iota(jnp.int32, (heads, blocks), 0)
    pair = head * shard_blocks + jnp.bitwise_and(key_block, shard_blocks - 1)
    low = jnp.min(jnp.where(needed > 0, pair, heads * shard_blocks), axis=0, keepdims=True)
    owner = lax.broadcasted_iota(jnp.int32, (shards, blocks), 1) >> shift_of(shard_blocks)
    mine = owner == lax.broadcasted_iota(jnp.int32, (shards, blocks), 0)
    low_col = jnp.min(jnp.where(mine, low, heads * shard_blocks), axis=1, keepdims=True)
    return pair, mine, low_col


def request_kernel(mask_ref, table_ref):
    heads, shard_blocks, _ = mask_ref.shape
    needed = jnp.max(mask_ref[...], axis=1)
    pair, mine, low_col = slot_lows(needed, shard_blocks)
    high = jnp.max(jnp.where(needed > 0, pair, -1), axis=0, keepdims=True)
    high_col = jnp.max(jnp.where(mine, high, -1), axis=1, keepdims=True)
    high_col = jnp.where(high_col == low_col, -1, high_col)
    low_col = jnp.where(low_col == heads * shard_blocks, -1, low_col)
    lane = lax.broadcasted_iota(jnp.int32, table_ref.shape, 1)
    table_ref[...] = jnp.where(lane == 0, low_col, high_col)


def local_tokens(perm, rows):
    return jnp.bitwise_and(perm + lax.axis_index("head") * (rows // 2), rows - 1)


def plan_kernel(mask_ref, position_ref, bias_ref):
    heads, shard_blocks, blocks = mask_ref.shape
    mask = mask_ref[...]
    needed = jnp.max(mask, axis=1)
    pair, mine, low_col = slot_lows(needed, shard_blocks)
    low_own = jnp.min(jnp.where(mine, low_col, heads * shard_blocks), axis=0, keepdims=True)
    key_block = lax.broadcasted_iota(jnp.int32, (heads, blocks), 1)
    slot = (key_block >> shift_of(shard_blocks)) * CAPACITY + (pair != low_own).astype(jnp.int32)
    upper = (
        lax.broadcasted_iota(jnp.int32, (blocks, blocks), 0)
        < lax.broadcasted_iota(jnp.int32, (blocks, blocks), 1)
    )
    prefix = jnp.dot(
        needed.astype(jnp.float32).astype(jnp.bfloat16),
        jnp.where(upper, 1.0, 0.0).astype(jnp.bfloat16),
        preferred_element_type=jnp.float32,
    )
    lane = lax.broadcasted_iota(jnp.int32, (heads, 128), 1)
    row = lax.broadcasted_iota(jnp.int32, (heads, 128), 0)
    position = jnp.zeros((heads, 128), jnp.int32)
    for j in range(PICKS):
        chosen = (needed > 0) & (prefix == float(j))
        slot_j = jnp.sum(jnp.where(chosen, slot, 0), axis=1, keepdims=True)
        position = jnp.where(lane == j, slot_j, position)
        bias = jnp.zeros((heads, 128), jnp.float32)
        for q in range(shard_blocks):
            live = jnp.max(jnp.where(chosen, mask[:, q, :], 0), axis=1, keepdims=True)
            bias = jnp.where((lane == row * shard_blocks + q) & (live == 0), MASKED, bias)
        bias_ref[j] = bias
    position_ref[...] = position


def sort_kernel(
    request_ref, perm_hbm, key_own, key_far, value_own, value_far,
    send_ref, member_ref, perm_raw, perm_pad, member_pad, buf, out_ref, sem, perm_sem, send_sem,
):
    heads, rows = perm_hbm.shape
    steps, _, half, step_width = buf.shape
    step_heads = step_width // HEAD_DIM
    shard_blocks = rows // BLOCK
    base = lax.axis_index("head") * (heads * HEAD_DIM)

    def copies(g):
        cut = pl.ds(pl.multiple_of(base + g * step_width, 128), step_width)
        return [
            pltpu.make_async_copy(ref.at[:, cut], buf.at[g, n], sem.at[g, n])
            for n, ref in enumerate((key_own, value_own, key_far, value_far))
        ]

    perm_copy = pltpu.make_async_copy(perm_hbm, perm_raw, perm_sem)
    perm_copy.start()
    for g in range(steps):
        for copy in copies(g):
            copy.start()
    pairs = heads * shard_blocks
    member_pad[pairs:, :] = jnp.zeros((member_pad.shape[0] - pairs, rows), jnp.float32)
    token = lax.broadcasted_iota(jnp.int32, (rows, half), 1)
    token = token.astype(jnp.float32).astype(jnp.bfloat16)
    perm_copy.wait()
    perm_pad[0:heads, :] = perm_raw[...]
    column = jnp.transpose(local_tokens(perm_pad[...], rows))
    own_column = jnp.where(column < half, column, -1).astype(jnp.float32)
    far_column = jnp.where(column < half, -1, column - half).astype(jnp.float32)

    def order_of(h):
        parts = []
        for table in (own_column, far_column):
            wide = jnp.broadcast_to(table[:, h : h + 1], (rows, 128)).astype(jnp.bfloat16)
            wide = jnp.tile(wide, (1, half // 128))
            parts.append(jnp.where(wide == token, jnp.bfloat16(1.0), jnp.bfloat16(0.0)))
        return jnp.concatenate(parts, axis=1)

    def block_sum(part):
        while part.shape[0] > 16:
            middle = part.shape[0] // 2
            part = part[:middle] + part[middle:]
        return jnp.sum(part.astype(jnp.float32), axis=0, keepdims=True)

    following = order_of(0)
    for h in range(heads):
        order = following
        if h + 1 < heads:
            following = order_of(h + 1)
        g, k = divmod(h, step_heads)
        if k == 0:
            for copy in copies(g):
                copy.wait()
        cut = slice(k * HEAD_DIM, (k + 1) * HEAD_DIM)
        own = jnp.concatenate([buf[g, 0, :, cut], buf[g, 1, :, cut]], axis=1)
        far = jnp.concatenate([buf[g, 2, :, cut], buf[g, 3, :, cut]], axis=1)
        ordered = jnp.dot(
            order, jnp.concatenate([own, far], axis=0), preferred_element_type=jnp.float32
        ).astype(jnp.bfloat16)
        for b in range(shard_blocks):
            part = slice(b * BLOCK, (b + 1) * BLOCK)
            row = h * shard_blocks + b
            member_pad[row : row + 1, :] = block_sum(order[part])
            out_ref[row, 0:BLOCK] = ordered[part, :HEAD_DIM]
            out_ref[row, BLOCK : 2 * BLOCK] = ordered[part, HEAD_DIM:]

    def start(d, count):
        for j in range(CAPACITY):
            asked = request_ref[d, j]

            @pl.when(asked >= 0)
            def _():
                pltpu.make_async_copy(
                    out_ref.at[asked], send_ref.at[d * CAPACITY + j], send_sem
                ).start()

            count = count + (asked >= 0).astype(jnp.int32)
        return count

    started = lax.fori_loop(0, request_ref.shape[0], start, jnp.int32(0), unroll=8)
    member_ref[...] = jnp.transpose(member_pad[...]).astype(jnp.bfloat16)

    def finish(n, carry):
        pltpu.make_async_copy(out_ref.at[0], send_ref.at[0], send_sem).wait()
        return carry

    lax.fori_loop(0, started, finish, 0)


def score(h, query, member, bias_ref, blocks_ref):
    left = jnp.concatenate([query, member], axis=1)
    keys = []
    for j in range(PICKS):
        bias = jnp.broadcast_to(bias_ref[j, h : h + 1, :].astype(jnp.bfloat16), (BLOCK, 128))
        keys.append(jnp.concatenate([blocks_ref[h * PICKS + j, 0:BLOCK], bias], axis=1))
    return lax.dot_general(
        left,
        jnp.concatenate(keys, axis=0),
        (((1,), (1,)), ((), ())),
        preferred_element_type=jnp.float32,
    )


def mix(h, scores, blocks_ref):
    top = jnp.max(scores, axis=1, keepdims=True)
    exponent = jnp.exp2((scores - top) * (math.log2(math.e) / math.sqrt(HEAD_DIM)))
    weights = exponent.astype(jnp.bfloat16)
    values = jnp.concatenate(
        [blocks_ref[h * PICKS + j, BLOCK : 2 * BLOCK] for j in range(PICKS)], axis=0
    )
    ones = jnp.ones((PICKS * BLOCK, HEAD_DIM), jnp.bfloat16)
    mixed = jnp.dot(
        weights, jnp.concatenate([values, ones], axis=1), preferred_element_type=jnp.float32
    )
    return (mixed[:, :HEAD_DIM] / mixed[:, HEAD_DIM:]).astype(jnp.bfloat16)


def attend(heads, ready, query_ref, member, bias_ref, blocks_ref, finish):
    def score_of(h):
        ready(h)
        cut = slice(h * HEAD_DIM, (h + 1) * HEAD_DIM)
        return score(h, query_ref[:, cut], member, bias_ref, blocks_ref)

    following = score_of(0)
    for h in range(heads):
        scores = following
        if h + 1 < heads:
            following = score_of(h + 1)
        finish(h, mix(h, scores, blocks_ref))


def query_copies(query_hbm, query_ref, sem):
    width = query_ref.shape[1]
    count = sem.shape[0]
    base = lax.axis_index("head") * width
    step_width = width // count
    return [
        pltpu.make_async_copy(
            query_hbm.at[:, pl.ds(pl.multiple_of(base + g * step_width, 128), step_width)],
            query_ref.at[:, g * step_width : (g + 1) * step_width],
            sem.at[g],
        )
        for g in range(count)
    ]


def far_kernel(
    position_ref, member_ref, bias_ref, query_hbm, got_ref,
    out_ref, blocks_ref, query_ref, sem, query_sem,
):
    heads = position_ref.shape[0]
    half = out_ref.shape[0]
    group = heads // sem.shape[0]
    loads = query_copies(query_hbm, query_ref, query_sem)

    def start(h, carry):
        for j in range(PICKS):
            pltpu.make_async_copy(
                got_ref.at[position_ref[h, j]], blocks_ref.at[h * PICKS + j], sem.at[h // group]
            ).start()
        return carry

    for h in range(group):
        start(h, 0)
    for load in loads:
        load.start()
    for h in range(group, heads):
        start(h, 0)
    for load in loads:
        load.wait()

    def ready(h):
        if h % group == 0:
            part = blocks_ref.at[h * PICKS : (h + group) * PICKS]
            pltpu.make_async_copy(part, part, sem.at[h // group]).wait()

    def finish(h, mixed):
        out_ref[:, h * HEAD_DIM : (h + 1) * HEAD_DIM] = mixed

    attend(heads, ready, query_ref, member_ref[half:, :], bias_ref, blocks_ref, finish)


def own_kernel(
    member_ref, bias_ref, blocks_ref, query_hbm, out_ref, query_ref, stage, sem, query_sem
):
    half, width = stage.shape
    heads = width // HEAD_DIM
    step_width = HEADS_STEP * HEAD_DIM
    base = lax.axis_index("head") * width
    loads = query_copies(query_hbm, query_ref, query_sem)
    for load in loads:
        load.start()

    def copy(g):
        return pltpu.make_async_copy(
            stage.at[:, g * step_width : (g + 1) * step_width],
            out_ref.at[:, pl.ds(pl.multiple_of(base + g * step_width, 128), step_width)],
            sem.at[g],
        )

    def finish(h, mixed):
        stage[:, h * HEAD_DIM : (h + 1) * HEAD_DIM] = mixed
        if h % HEADS_STEP == HEADS_STEP - 1:
            copy(h // HEADS_STEP).start()

    def ready(h):
        if h == 0:
            for load in loads:
                load.wait()

    attend(heads, ready, query_ref, member_ref[:half, :], bias_ref, blocks_ref, finish)
    for g in range(heads // HEADS_STEP):
        copy(g).wait()


def place_kernel(out_in, far_ref, out_ref, sem):
    del out_in
    width = far_ref.shape[1]
    start = pl.multiple_of((1 - lax.axis_index("head")) * width, 128)
    copy = pltpu.make_async_copy(far_ref, out_ref.at[:, pl.ds(start, width)], sem)
    copy.start()
    copy.wait()


def shards(queries, key_states, value_states, cluster_perm, block_mask):
    heads, rows = cluster_perm.shape
    half, columns = queries.shape
    width = heads * HEAD_DIM
    shard_blocks = rows // BLOCK
    seq_count = lax.axis_size("seq")
    pairs = heads * shard_blocks
    slots = seq_count * CAPACITY
    steps = heads // HEADS_STEP
    vmem = pl.BlockSpec(memory_space=pltpu.VMEM)
    smem = pl.BlockSpec(memory_space=pltpu.SMEM)
    hbm = pl.BlockSpec(memory_space=pltpu.HBM)
    limit = lambda mib: pltpu.CompilerParams(vmem_limit_bytes=mib << 20)
    held = lambda x: pltpu.with_memory_space_constraint(x, pltpu.VMEM)
    far = lambda x: pltpu.with_memory_space_constraint(x, pltpu.HBM)
    held_out = lambda shape, dtype: pltpu.VMEM(shape, dtype)
    hbm_out = lambda shape, dtype: pltpu.HBM(shape, dtype)
    dma = pltpu.SemaphoreType.DMA
    bf16 = jnp.bfloat16

    table = pl.pallas_call(
        request_kernel,
        out_shape=jax.ShapeDtypeStruct((seq_count, 128), jnp.int32),
        in_specs=[vmem],
        out_specs=vmem,
        name="request",
    )(block_mask)
    requested = lax.all_to_all(
        table.reshape(seq_count, 1, 128), "seq", split_axis=0, concat_axis=0, tiled=True
    ).reshape(seq_count, 128)

    def swap(x):
        return lax.ppermute(x, "head", [(0, 1), (1, 0)])

    key_far = swap(key_states)
    value_far = swap(value_states)

    query_far = swap(queries)
    position, bias = pl.pallas_call(
        plan_kernel,
        out_shape=[
            jax.ShapeDtypeStruct((heads, 128), jnp.int32),
            jax.ShapeDtypeStruct((PICKS, heads, 128), jnp.float32),
        ],
        in_specs=[vmem],
        out_specs=[vmem] * 2,
        name="plan",
    )(block_mask)
    send, member = pl.pallas_call(
        sort_kernel,
        out_shape=[
            hbm_out((slots, 2 * BLOCK, HEAD_DIM), bf16),
            held_out((rows, 128), bf16),
        ],
        in_specs=[smem, hbm, hbm, hbm, hbm, hbm],
        out_specs=[hbm, vmem],
        scratch_shapes=[
            pltpu.VMEM((heads, rows), jnp.int32),
            pltpu.VMEM((128, rows), jnp.int32),
            pltpu.VMEM((128, rows), jnp.float32),
            pltpu.VMEM((heads // SORT_STEP, 4, half, SORT_STEP * HEAD_DIM), bf16),
            pltpu.VMEM((pairs, 2 * BLOCK, HEAD_DIM), bf16),
            dma((heads // SORT_STEP, 4)),
            dma,
            dma,
        ],
        compiler_params=limit(32),
        name="sort",
    )(requested, far(cluster_perm), far(key_states), key_far, far(value_states), value_far)
    send, member, position, bias, query_far = lax.optimization_barrier(
        (send, member, position, bias, query_far)
    )
    got = lax.all_to_all(send, "seq", split_axis=0, concat_axis=0, tiled=True)

    out_far, picked = pl.pallas_call(
        far_kernel,
        out_shape=[
            held_out((half, width), bf16),
            held_out((pairs, 2 * BLOCK, HEAD_DIM), bf16),
        ],
        in_specs=[smem, vmem, vmem, hbm, hbm],
        out_specs=[vmem, vmem],
        scratch_shapes=[pltpu.VMEM((half, width), bf16), dma((GATHERS,)), dma((1,))],
        compiler_params=limit(32),
        name="far_rows",
    )(position, held(member), bias, query_far, far(got))
    out_far = swap(out_far)
    out_own = pl.pallas_call(
        own_kernel,
        out_shape=hbm_out((half, columns), bf16),
        in_specs=[vmem, vmem, vmem, hbm],
        out_specs=hbm,
        scratch_shapes=[
            pltpu.VMEM((half, width), bf16),
            pltpu.VMEM((half, width), bf16),
            dma((steps,)),
            dma((1,)),
        ],
        compiler_params=limit(32),
        name="own_rows",
    )(held(member), bias, held(picked), far(queries))
    return pl.pallas_call(
        place_kernel,
        out_shape=hbm_out((half, columns), bf16),
        in_specs=[hbm, vmem],
        out_specs=hbm,
        scratch_shapes=[dma],
        input_output_aliases={0: 0},
        name="place",
    )(out_own, held(out_far))


def solution(mesh):
    placed = (
        P(("seq", "head"), None),
        P(("seq", "head"), None),
        P(("seq", "head"), None),
        P("head", "seq"),
        P("head", "seq", None),
    )
    return jax.shard_map(
        shards, mesh=mesh, in_specs=placed, out_specs=P(("seq", "head"), None), check_vma=False
    )
```

```python
import functools
import math

import jax
import jax.numpy as jnp
from jax import lax
from jax.experimental import pallas as pl
from jax.experimental.pallas import tpu as pltpu
from jax.sharding import PartitionSpec as P

HEAD_DIM = 128
BLOCK = 128
CAPACITY = 2
PICKS = 4
EARLY = 8
SORT_STEP = 6
LAST = 6
MASKED = -1e30


def shift_of(count):
    return count.bit_length() - 1


def slot_lows(needed, shard_blocks):
    heads, blocks = needed.shape
    shards = blocks // shard_blocks
    key_block = lax.broadcasted_iota(jnp.int32, (heads, blocks), 1)
    head = lax.broadcasted_iota(jnp.int32, (heads, blocks), 0)
    pair = head * shard_blocks + jnp.bitwise_and(key_block, shard_blocks - 1)
    low = jnp.min(jnp.where(needed > 0, pair, heads * shard_blocks), axis=0, keepdims=True)
    owner = lax.broadcasted_iota(jnp.int32, (shards, blocks), 1) >> shift_of(shard_blocks)
    mine = owner == lax.broadcasted_iota(jnp.int32, (shards, blocks), 0)
    low_col = jnp.min(jnp.where(mine, low, heads * shard_blocks), axis=1, keepdims=True)
    return pair, mine, low_col


def request_kernel(mask_ref, table_ref):
    heads, shard_blocks, _ = mask_ref.shape
    needed = jnp.max(mask_ref[...], axis=1)
    pair, mine, low_col = slot_lows(needed, shard_blocks)
    high = jnp.max(jnp.where(needed > 0, pair, -1), axis=0, keepdims=True)
    high_col = jnp.max(jnp.where(mine, high, -1), axis=1, keepdims=True)
    high_col = jnp.where(high_col == low_col, -1, high_col)
    low_col = jnp.where(low_col == heads * shard_blocks, -1, low_col)
    lane = lax.broadcasted_iota(jnp.int32, table_ref.shape, 1)
    table_ref[...] = jnp.where(lane == 0, low_col, high_col)


def local_tokens(perm, rows):
    return jnp.bitwise_and(perm + lax.axis_index("head") * (rows // 2), rows - 1)


def plan_kernel(mask_ref, position_ref, bias_ref):
    heads, shard_blocks, blocks = mask_ref.shape
    mask = mask_ref[...]
    needed = jnp.max(mask, axis=1)
    pair, mine, low_col = slot_lows(needed, shard_blocks)
    low_own = jnp.min(jnp.where(mine, low_col, heads * shard_blocks), axis=0, keepdims=True)
    key_block = lax.broadcasted_iota(jnp.int32, (heads, blocks), 1)
    slot = (key_block >> shift_of(shard_blocks)) * CAPACITY + (pair != low_own).astype(jnp.int32)
    upper = (
        lax.broadcasted_iota(jnp.int32, (blocks, blocks), 0)
        < lax.broadcasted_iota(jnp.int32, (blocks, blocks), 1)
    )
    prefix = jnp.dot(
        needed.astype(jnp.float32).astype(jnp.bfloat16),
        jnp.where(upper, 1.0, 0.0).astype(jnp.bfloat16),
        preferred_element_type=jnp.float32,
    )
    lane = lax.broadcasted_iota(jnp.int32, (heads, 128), 1)
    row = lax.broadcasted_iota(jnp.int32, (heads, 128), 0)
    position = jnp.zeros((heads, 128), jnp.int32)
    for j in range(PICKS):
        chosen = (needed > 0) & (prefix == float(j))
        slot_j = jnp.sum(jnp.where(chosen, slot, 0), axis=1, keepdims=True)
        position = jnp.where(lane == j, slot_j, position)
        bias = jnp.zeros((heads, 128), jnp.float32)
        for q in range(shard_blocks):
            live = jnp.max(jnp.where(chosen, mask[:, q, :], 0), axis=1, keepdims=True)
            bias = jnp.where((lane == row * shard_blocks + q) & (live == 0), MASKED, bias)
        bias_ref[j] = bias
    position_ref[...] = position


def sort_heads(
    first, perm_hbm, sources, out_ref, member_pad, perm_raw, perm_pad, buf, sem, perm_sem
):
    heads, rows = perm_hbm.shape
    steps, _, half, step_width = buf.shape
    step_heads = step_width // HEAD_DIM
    count = steps * step_heads
    shard_blocks = rows // BLOCK
    base = (lax.axis_index("head") * heads + first) * HEAD_DIM

    def copies(g):
        cut = pl.ds(pl.multiple_of(base + g * step_width, 128), step_width)
        return [
            pltpu.make_async_copy(ref.at[:, cut], buf.at[g, n], sem.at[g, n])
            for n, ref in enumerate(sources)
        ]

    perm_copy = pltpu.make_async_copy(perm_hbm, perm_raw, perm_sem)
    perm_copy.start()
    for g in range(steps):
        for copy in copies(g):
            copy.start()
    member_pad[...] = jnp.zeros(member_pad.shape, jnp.float32)
    token = lax.broadcasted_iota(jnp.int32, (rows, half), 1)
    token = token.astype(jnp.float32).astype(jnp.bfloat16)
    perm_copy.wait()
    perm_pad[0:heads, :] = perm_raw[...]
    column = jnp.transpose(local_tokens(perm_pad[...], rows))
    own_column = jnp.where(column < half, column, -1).astype(jnp.float32)
    far_column = jnp.where(column < half, -1, column - half).astype(jnp.float32)

    def order_of(h):
        parts = []
        for table in (own_column, far_column):
            wide = jnp.broadcast_to(table[:, h : h + 1], (rows, 128)).astype(jnp.bfloat16)
            wide = jnp.tile(wide, (1, half // 128))
            parts.append(jnp.where(wide == token, jnp.bfloat16(1.0), jnp.bfloat16(0.0)))
        return jnp.concatenate(parts, axis=1)

    def block_sum(part):
        while part.shape[0] > 16:
            middle = part.shape[0] // 2
            part = part[:middle] + part[middle:]
        return jnp.sum(part.astype(jnp.float32), axis=0, keepdims=True)

    following = order_of(first)
    for n in range(count):
        order = following
        if n + 1 < count:
            following = order_of(first + n + 1)
        g, k = divmod(n, step_heads)
        if k == 0:
            for copy in copies(g):
                copy.wait()
        cut = slice(k * HEAD_DIM, (k + 1) * HEAD_DIM)
        own = jnp.concatenate([buf[g, 0, :, cut], buf[g, 1, :, cut]], axis=1)
        far = jnp.concatenate([buf[g, 2, :, cut], buf[g, 3, :, cut]], axis=1)
        ordered = jnp.dot(
            order, jnp.concatenate([own, far], axis=0), preferred_element_type=jnp.float32
        ).astype(jnp.bfloat16)
        for b in range(shard_blocks):
            part = slice(b * BLOCK, (b + 1) * BLOCK)
            row = (first + n) * shard_blocks + b
            member_pad[row : row + 1, :] = block_sum(order[part])
            slot = n * shard_blocks + b
            out_ref[slot, 0:BLOCK] = ordered[part, :HEAD_DIM]
            out_ref[slot, BLOCK : 2 * BLOCK] = ordered[part, HEAD_DIM:]
    return jnp.transpose(member_pad[...])


def early_kernel(
    perm_hbm, key_own, key_far, value_own, value_far,
    early_ref, member_ref, perm_raw, perm_pad, member_pad, buf, blocks, sem, perm_sem, out_sem,
):
    sources = (key_own, value_own, key_far, value_far)
    member = sort_heads(
        0, perm_hbm, sources, blocks, member_pad, perm_raw, perm_pad, buf, sem, perm_sem
    )
    copy = pltpu.make_async_copy(blocks, early_ref, out_sem)
    copy.start()
    member_ref[...] = member.astype(jnp.bfloat16)
    copy.wait()


def sort_kernel(
    request_ref, perm_hbm, key_own, key_far, value_own, value_far, early_ref, early_member,
    send_ref, member_ref, perm_raw, perm_pad, member_pad, buf, blocks,
    sem, perm_sem, early_sem, send_sem,
):
    early_count = early_ref.shape[0]
    early_copy = pltpu.make_async_copy(early_ref, blocks.at[0:early_count], early_sem)
    early_copy.start()
    sources = (key_own, value_own, key_far, value_far)
    member = sort_heads(
        EARLY, perm_hbm, sources, blocks.at[early_count:], member_pad, perm_raw, perm_pad,
        buf, sem, perm_sem,
    )
    early_copy.wait()

    def start(d, count):
        for j in range(CAPACITY):
            asked = request_ref[d, j]

            @pl.when(asked >= 0)
            def _():
                pltpu.make_async_copy(
                    blocks.at[asked], send_ref.at[d * CAPACITY + j], send_sem
                ).start()

            count = count + (asked >= 0).astype(jnp.int32)
        return count

    started = lax.fori_loop(0, request_ref.shape[0], start, jnp.int32(0), unroll=8)
    member_ref[...] = (member + early_member[...].astype(jnp.float32)).astype(jnp.bfloat16)

    def finish(n, carry):
        pltpu.make_async_copy(blocks.at[0], send_ref.at[0], send_sem).wait()
        return carry

    lax.fori_loop(0, started, finish, 0)


def score(h, query, member, bias_ref, blocks):
    keys = []
    for j in range(PICKS):
        bias = jnp.broadcast_to(bias_ref[j, h : h + 1, :].astype(jnp.bfloat16), (BLOCK, 128))
        keys.append(jnp.concatenate([blocks[j, 0:BLOCK], bias], axis=1))
    return lax.dot_general(
        jnp.concatenate([query, member], axis=1),
        jnp.concatenate(keys, axis=0),
        (((1,), (1,)), ((), ())),
        preferred_element_type=jnp.float32,
    )


def mix(scores, blocks):
    top = jnp.max(scores, axis=1, keepdims=True)
    exponent = jnp.exp2((scores - top) * (math.log2(math.e) / math.sqrt(HEAD_DIM)))
    weights = exponent.astype(jnp.bfloat16)
    values = jnp.concatenate([blocks[j, BLOCK : 2 * BLOCK] for j in range(PICKS)], axis=0)
    ones = jnp.ones((PICKS * BLOCK, HEAD_DIM), jnp.bfloat16)
    mixed = jnp.dot(
        weights, jnp.concatenate([values, ones], axis=1), preferred_element_type=jnp.float32
    )
    return (mixed[:, :HEAD_DIM] / mixed[:, HEAD_DIM:]).astype(jnp.bfloat16)


def attend(first, count, query_ref, member, bias_ref, blocks_ref, far_ref, stage, send_own):
    half = stage.shape[0]
    blocks_of = lambda n: blocks_ref.at[n * PICKS : (n + 1) * PICKS]

    def score_of(n):
        cut = slice(n * HEAD_DIM, (n + 1) * HEAD_DIM)
        return score(first + n, query_ref[:, cut], member, bias_ref, blocks_of(n))

    following = score_of(0)
    for n in range(count):
        scores = following
        if n + 1 < count:
            following = score_of(n + 1)
        mixed = mix(scores, blocks_of(n))
        cut = slice(n * HEAD_DIM, (n + 1) * HEAD_DIM)
        stage[:, cut] = mixed[:half]
        far_ref[:, cut] = mixed[half:]
        send_own(n)


def own_copies(first, stage, out_ref, sem):
    pieces = sem.shape[0]
    step = stage.shape[1] // pieces
    base = lax.axis_index("head") * (out_ref.shape[1] // 2) + first * HEAD_DIM
    copies = [
        pltpu.make_async_copy(
            stage.at[:, g * step : (g + 1) * step],
            out_ref.at[:, pl.ds(pl.multiple_of(base + g * step, 128), step)],
            sem.at[g],
        )
        for g in range(pieces)
    ]

    def send_own(n):
        g, rest = divmod((n + 1) * HEAD_DIM, step)
        if rest == 0:
            copies[g - 1].start()

    return copies, send_own


def first_kernel(
    position_ref, member_ref, bias_ref, query_own, query_far, got_ref,
    out_ref, far_ref, later_blocks, later_query,
    blocks, query, stage, block_sem, query_sem, out_sem,
):
    heads = position_ref.shape[0]
    half = stage.shape[0]
    count = stage.shape[1] // HEAD_DIM
    width = heads * HEAD_DIM
    base = lax.axis_index("head") * width

    def query_copies(first, target, n):
        cut = pl.ds(pl.multiple_of(base + first * HEAD_DIM, 128), target.shape[1])
        return [
            pltpu.make_async_copy(
                source.at[:, cut], target.at[r * half : (r + 1) * half], query_sem.at[n, r]
            )
            for r, source in enumerate((query_own, query_far))
        ]

    def block_copy(h, j):
        target = blocks.at[h * PICKS + j] if h < count else later_blocks.at[(h - count) * PICKS + j]
        return pltpu.make_async_copy(
            got_ref.at[position_ref[h, j]], target, block_sem.at[0 if h < count else 1]
        )

    now, later = query_copies(0, query, 0), query_copies(count, later_query, 1)
    for copy in now:
        copy.start()
    for h in range(count):
        for j in range(PICKS):
            block_copy(h, j).start()
    for copy in later:
        copy.start()
    for h in range(count, heads):
        for j in range(PICKS):
            block_copy(h, j).start()
    for copy in now:
        copy.wait()
    pltpu.make_async_copy(blocks, blocks, block_sem.at[0]).wait()
    copies, send_own = own_copies(0, stage, out_ref, out_sem)
    attend(0, count, query, member_ref[...], bias_ref, blocks, far_ref, stage, send_own)
    for copy in later:
        copy.wait()
    pltpu.make_async_copy(later_blocks, later_blocks, block_sem.at[1]).wait()
    for copy in copies:
        copy.wait()


def last_kernel(
    member_ref, bias_ref, blocks, query, out_in, out_ref, far_ref, stage, out_sem
):
    del out_in
    count = stage.shape[1] // HEAD_DIM
    first = bias_ref.shape[1] - count
    copies, send_own = own_copies(first, stage, out_ref, out_sem)
    attend(first, count, query, member_ref[...], bias_ref, blocks, far_ref, stage, send_own)
    for copy in copies:
        copy.wait()


def place_kernel(first, out_in, far_ref, out_ref, sem):
    del out_in
    width = far_ref.shape[1]
    start = (1 - lax.axis_index("head")) * (out_ref.shape[1] // 2) + first * HEAD_DIM
    copy = pltpu.make_async_copy(
        far_ref, out_ref.at[:, pl.ds(pl.multiple_of(start, 128), width)], sem
    )
    copy.start()
    copy.wait()


def shards(queries, key_states, value_states, cluster_perm, block_mask):
    heads, rows = cluster_perm.shape
    half, columns = queries.shape
    width = heads * HEAD_DIM
    shard_blocks = rows // BLOCK
    seq_count = lax.axis_size("seq")
    pairs = heads * shard_blocks
    slots = seq_count * CAPACITY
    vmem = pl.BlockSpec(memory_space=pltpu.VMEM)
    smem = pl.BlockSpec(memory_space=pltpu.SMEM)
    hbm = pl.BlockSpec(memory_space=pltpu.HBM)
    limit = lambda mib: pltpu.CompilerParams(vmem_limit_bytes=mib << 20)
    held = lambda x: pltpu.with_memory_space_constraint(x, pltpu.VMEM)
    far = lambda x: pltpu.with_memory_space_constraint(x, pltpu.HBM)
    held_out = lambda shape, dtype: pltpu.VMEM(shape, dtype)
    hbm_out = lambda shape, dtype: pltpu.HBM(shape, dtype)
    dma = pltpu.SemaphoreType.DMA
    bf16 = jnp.bfloat16

    table = pl.pallas_call(
        request_kernel,
        out_shape=jax.ShapeDtypeStruct((seq_count, 128), jnp.int32),
        in_specs=[vmem],
        out_specs=vmem,
        name="request",
    )(block_mask)
    requested = lax.all_to_all(
        table.reshape(seq_count, 1, 128), "seq", split_axis=0, concat_axis=0, tiled=True
    ).reshape(seq_count, 128)

    def swap(x):
        return lax.ppermute(x, "head", [(0, 1), (1, 0)])

    key_far = swap(key_states)
    value_far = swap(value_states)

    query_far = swap(queries)
    position, bias = pl.pallas_call(
        plan_kernel,
        out_shape=[
            jax.ShapeDtypeStruct((heads, 128), jnp.int32),
            jax.ShapeDtypeStruct((PICKS, heads, 128), jnp.float32),
        ],
        in_specs=[vmem],
        out_specs=[vmem] * 2,
        name="plan",
    )(block_mask)
    key_args = (far(cluster_perm), far(key_states), key_far, far(value_states), value_far)

    def sort_scratch(count, step, kept):
        return [
            pltpu.VMEM((heads, rows), jnp.int32),
            pltpu.VMEM((128, rows), jnp.int32),
            pltpu.VMEM((128, rows), jnp.float32),
            pltpu.VMEM((count // step, 4, half, step * HEAD_DIM), bf16),
            pltpu.VMEM((kept, 2 * BLOCK, HEAD_DIM), bf16),
            dma((count // step, 4)),
            dma,
        ]

    early, early_member = pl.pallas_call(
        early_kernel,
        out_shape=[
            hbm_out((EARLY * shard_blocks, 2 * BLOCK, HEAD_DIM), bf16),
            jax.ShapeDtypeStruct((rows, 128), bf16),
        ],
        in_specs=[hbm] * 5,
        out_specs=[hbm, vmem],
        scratch_shapes=sort_scratch(EARLY, EARLY, EARLY * shard_blocks) + [dma],
        compiler_params=limit(24),
        name="early_sort",
    )(*key_args)
    send, member = pl.pallas_call(
        sort_kernel,
        out_shape=[
            hbm_out((slots, 2 * BLOCK, HEAD_DIM), bf16),
            held_out((rows, 128), bf16),
        ],
        in_specs=[smem] + [hbm] * 6 + [vmem],
        out_specs=[hbm, vmem],
        scratch_shapes=sort_scratch(heads - EARLY, SORT_STEP, pairs) + [dma, dma],
        compiler_params=limit(32),
        name="sort",
    )(requested, *key_args, far(early), early_member)
    send, member, position, bias, query_far = lax.optimization_barrier(
        (send, member, position, bias, query_far)
    )
    got = lax.all_to_all(send, "seq", split_axis=0, concat_axis=0, tiled=True)

    first, last = heads - LAST, LAST
    out, far_first, later_blocks, later_query = pl.pallas_call(
        first_kernel,
        out_shape=[
            hbm_out((half, columns), bf16),
            held_out((half, first * HEAD_DIM), bf16),
            held_out((last * PICKS, 2 * BLOCK, HEAD_DIM), bf16),
            held_out((rows, last * HEAD_DIM), bf16),
        ],
        in_specs=[smem, vmem, vmem, hbm, hbm, hbm],
        out_specs=[hbm, vmem, vmem, vmem],
        scratch_shapes=[
            pltpu.VMEM((first * PICKS, 2 * BLOCK, HEAD_DIM), bf16),
            pltpu.VMEM((rows, first * HEAD_DIM), bf16),
            pltpu.VMEM((half, first * HEAD_DIM), bf16),
            dma((2,)),
            dma((2, 2)),
            dma((2,)),
        ],
        compiler_params=limit(32),
        name="first_heads",
    )(position, held(member), bias, far(queries), query_far, far(got))
    far_first = swap(far_first)
    out, far_last = pl.pallas_call(
        last_kernel,
        out_shape=[
            hbm_out((half, columns), bf16),
            held_out((half, last * HEAD_DIM), bf16),
        ],
        in_specs=[vmem, vmem, vmem, vmem, hbm],
        out_specs=[hbm, vmem],
        scratch_shapes=[pltpu.VMEM((half, last * HEAD_DIM), bf16), dma((1,))],
        input_output_aliases={4: 0},
        compiler_params=limit(32),
        name="last_heads",
    )(held(member), bias, held(later_blocks), held(later_query), out)
    far_last = swap(far_last)

    def place(out, part, at):
        return pl.pallas_call(
            functools.partial(place_kernel, at),
            out_shape=hbm_out((half, columns), bf16),
            in_specs=[hbm, vmem],
            out_specs=hbm,
            scratch_shapes=[dma],
            input_output_aliases={0: 0},
            compiler_params=limit(8),
            name="place",
        )(out, held(part))

    return place(place(out, far_first, 0), far_last, first)


def solution(mesh):
    placed = (
        P(("seq", "head"), None),
        P(("seq", "head"), None),
        P(("seq", "head"), None),
        P("head", "seq"),
        P("head", "seq", None),
    )
    return jax.shard_map(
        shards, mesh=mesh, in_specs=placed, out_specs=P(("seq", "head"), None), check_vma=False
    )
```

```python
import math

import jax
import jax.numpy as jnp
from jax import lax
from jax.experimental import pallas as pl
from jax.experimental.pallas import tpu as pltpu
from jax.sharding import PartitionSpec as P

HEAD_DIM = 128
BLOCK = 128
CAPACITY = 2
PICKS = 4
EARLY = 8
SORT_STEP = 6
LAST = 6
MASKED = -1e30


def shift_of(count):
    return count.bit_length() - 1


def slot_lows(needed, shard_blocks):
    heads, blocks = needed.shape
    shards = blocks // shard_blocks
    key_block = lax.broadcasted_iota(jnp.int32, (heads, blocks), 1)
    head = lax.broadcasted_iota(jnp.int32, (heads, blocks), 0)
    pair = head * shard_blocks + jnp.bitwise_and(key_block, shard_blocks - 1)
    low = jnp.min(jnp.where(needed > 0, pair, heads * shard_blocks), axis=0, keepdims=True)
    owner = lax.broadcasted_iota(jnp.int32, (shards, blocks), 1) >> shift_of(shard_blocks)
    mine = owner == lax.broadcasted_iota(jnp.int32, (shards, blocks), 0)
    low_col = jnp.min(jnp.where(mine, low, heads * shard_blocks), axis=1, keepdims=True)
    return pair, mine, low_col


def request_kernel(mask_ref, table_ref):
    heads, shard_blocks, blocks = mask_ref.shape
    shards = blocks >> shift_of(shard_blocks)
    count = heads * shard_blocks
    mask = mask_ref[...]
    head = lax.broadcasted_iota(jnp.int32, mask.shape, 0)
    key_block = lax.broadcasted_iota(jnp.int32, mask.shape, 2)
    pair = head * shard_blocks + jnp.bitwise_and(key_block, shard_blocks - 1)
    low = jnp.min(jnp.where(mask > 0, pair, count), axis=0)
    high = jnp.max(jnp.where(mask > 0, pair, -1), axis=0)
    low = jnp.min(low, axis=0, keepdims=True)
    high = jnp.max(high, axis=0, keepdims=True)
    owner = lax.broadcasted_iota(jnp.int32, (shards, blocks), 1) >> shift_of(shard_blocks)
    mine = owner == lax.broadcasted_iota(jnp.int32, (shards, blocks), 0)
    low_col = jnp.min(jnp.where(mine, low, count), axis=1, keepdims=True)
    high_col = jnp.max(jnp.where(mine, high, -1), axis=1, keepdims=True)
    high_col = jnp.where(high_col == low_col, -1, high_col)
    low_col = jnp.where(low_col == count, -1, low_col)
    lane = lax.broadcasted_iota(jnp.int32, table_ref.shape, 1)
    table_ref[...] = jnp.where(lane == 0, low_col, high_col)


def local_tokens(perm, rows):
    return jnp.bitwise_and(perm + lax.axis_index("head") * (rows // 2), rows - 1)


def plan_kernel(mask_ref, position_ref, bias_ref):
    heads, shard_blocks, blocks = mask_ref.shape
    mask = mask_ref[...]
    needed = jnp.max(mask, axis=1)
    pair, mine, low_col = slot_lows(needed, shard_blocks)
    low_own = jnp.min(jnp.where(mine, low_col, heads * shard_blocks), axis=0, keepdims=True)
    key_block = lax.broadcasted_iota(jnp.int32, (heads, blocks), 1)
    slot = (key_block >> shift_of(shard_blocks)) * CAPACITY + (pair != low_own).astype(jnp.int32)
    upper = (
        lax.broadcasted_iota(jnp.int32, (blocks, blocks), 0)
        < lax.broadcasted_iota(jnp.int32, (blocks, blocks), 1)
    )
    prefix = jnp.dot(
        needed.astype(jnp.float32).astype(jnp.bfloat16),
        jnp.where(upper, 1.0, 0.0).astype(jnp.bfloat16),
        preferred_element_type=jnp.float32,
    )
    lane = lax.broadcasted_iota(jnp.int32, (heads, 128), 1)
    row = lax.broadcasted_iota(jnp.int32, (heads, 128), 0)
    position = jnp.zeros((heads, 128), jnp.int32)
    for j in range(PICKS):
        chosen = (needed > 0) & (prefix == float(j))
        slot_j = jnp.sum(jnp.where(chosen, slot, 0), axis=1, keepdims=True)
        position = jnp.where(lane == j, slot_j, position)
        bias = jnp.zeros((heads, 128), jnp.float32)
        for q in range(shard_blocks):
            live = jnp.max(jnp.where(chosen, mask[:, q, :], 0), axis=1, keepdims=True)
            bias = jnp.where((lane == row * shard_blocks + q) & (live == 0), MASKED, bias)
        bias_ref[j] = bias
    position_ref[...] = position


def sort_heads(first, heads, sources, column_of, out_ref, member_pad, buf, sem):
    steps, _, half, step_width = buf.shape
    rows = 2 * half
    step_heads = step_width // HEAD_DIM
    count = steps * step_heads
    shard_blocks = rows // BLOCK
    base = (lax.axis_index("head") * heads + first) * HEAD_DIM

    def copies(g):
        cut = pl.ds(pl.multiple_of(base + g * step_width, 128), step_width)
        return [
            pltpu.make_async_copy(ref.at[:, cut], buf.at[g, n], sem.at[g, n])
            for n, ref in enumerate(sources)
        ]

    for g in range(steps):
        for copy in copies(g):
            copy.start()
    member_pad[...] = jnp.zeros(member_pad.shape, jnp.float32)
    token = lax.broadcasted_iota(jnp.int32, (rows, half), 1)
    token = token.astype(jnp.float32).astype(jnp.bfloat16)
    column = column_of()
    own_column = jnp.where(column < half, column, -1).astype(jnp.float32)
    far_column = jnp.where(column < half, -1, column - half).astype(jnp.float32)

    def order_of(h):
        parts = []
        for table in (own_column, far_column):
            wide = jnp.broadcast_to(table[:, h : h + 1], (rows, 128)).astype(jnp.bfloat16)
            wide = jnp.tile(wide, (1, half // 128))
            parts.append(jnp.where(wide == token, jnp.bfloat16(1.0), jnp.bfloat16(0.0)))
        return jnp.concatenate(parts, axis=1)

    def block_sum(part):
        while part.shape[0] > 16:
            middle = part.shape[0] // 2
            part = part[:middle] + part[middle:]
        return jnp.sum(part.astype(jnp.float32), axis=0, keepdims=True)

    following = order_of(first)
    for n in range(count):
        order = following
        if n + 1 < count:
            following = order_of(first + n + 1)
        g, k = divmod(n, step_heads)
        if k == 0:
            for copy in copies(g):
                copy.wait()
        cut = slice(k * HEAD_DIM, (k + 1) * HEAD_DIM)
        own = jnp.concatenate([buf[g, 0, :, cut], buf[g, 1, :, cut]], axis=1)
        far = jnp.concatenate([buf[g, 2, :, cut], buf[g, 3, :, cut]], axis=1)
        ordered = jnp.dot(
            order, jnp.concatenate([own, far], axis=0), preferred_element_type=jnp.float32
        ).astype(jnp.bfloat16)
        for b in range(shard_blocks):
            part = slice(b * BLOCK, (b + 1) * BLOCK)
            row = (first + n) * shard_blocks + b
            member_pad[row : row + 1, :] = block_sum(order[part])
            slot = n * shard_blocks + b
            out_ref[slot, 0:BLOCK] = ordered[part, :HEAD_DIM]
            out_ref[slot, BLOCK : 2 * BLOCK] = ordered[part, HEAD_DIM:]
    return jnp.transpose(member_pad[...])


def early_kernel(
    perm_hbm, key_own, key_far, value_own, value_far,
    early_ref, member_ref, column_ref, perm_raw, perm_pad, member_pad, buf, blocks,
    sem, perm_sem, out_sem,
):
    heads, rows = perm_hbm.shape
    perm_copy = pltpu.make_async_copy(perm_hbm, perm_raw, perm_sem)
    perm_copy.start()

    def column_of():
        perm_copy.wait()
        perm_pad[0:heads, :] = perm_raw[...]
        column = jnp.transpose(local_tokens(perm_pad[...], rows))
        column_ref[...] = column
        return column

    sources = (key_own, value_own, key_far, value_far)
    member = sort_heads(0, heads, sources, column_of, blocks, member_pad, buf, sem)
    copy = pltpu.make_async_copy(blocks, early_ref, out_sem)
    copy.start()
    member_ref[...] = member.astype(jnp.bfloat16)
    copy.wait()


def sort_kernel(
    request_ref, column_ref, key_own, key_far, value_own, value_far, early_ref, early_member,
    send_ref, member_ref, member_pad, buf, blocks, sem, early_sem, send_sem,
):
    early_count = early_ref.shape[0]
    heads = blocks.shape[0] * BLOCK // column_ref.shape[0]
    sources = (key_own, value_own, key_far, value_far)
    early_copy = pltpu.make_async_copy(early_ref, blocks.at[0:early_count], early_sem)

    def column_of():
        early_copy.start()
        return column_ref[...]

    member = sort_heads(
        EARLY, heads, sources, column_of, blocks.at[early_count:], member_pad, buf, sem
    )
    early_copy.wait()

    def start(d, count):
        for j in range(CAPACITY):
            asked = request_ref[d, j]

            @pl.when(asked >= 0)
            def _():
                pltpu.make_async_copy(
                    blocks.at[asked], send_ref.at[d * CAPACITY + j], send_sem
                ).start()

            count = count + (asked >= 0).astype(jnp.int32)
        return count

    started = lax.fori_loop(0, request_ref.shape[0], start, jnp.int32(0), unroll=8)
    member_ref[...] = (member + early_member[...].astype(jnp.float32)).astype(jnp.bfloat16)

    def finish(n, carry):
        pltpu.make_async_copy(blocks.at[0], send_ref.at[0], send_sem).wait()
        return carry

    lax.fori_loop(0, started, finish, 0)


def score(h, query, member, bias_ref, blocks):
    keys = []
    for j in range(PICKS):
        bias = jnp.broadcast_to(bias_ref[j, h : h + 1, :].astype(jnp.bfloat16), (BLOCK, 128))
        keys.append(jnp.concatenate([blocks[j, 0:BLOCK], bias], axis=1))
    return lax.dot_general(
        jnp.concatenate([query, member], axis=1),
        jnp.concatenate(keys, axis=0),
        (((1,), (1,)), ((), ())),
        preferred_element_type=jnp.float32,
    )


def mix(scores, blocks):
    top = jnp.max(scores, axis=1, keepdims=True)
    exponent = jnp.exp2((scores - top) * (math.log2(math.e) / math.sqrt(HEAD_DIM)))
    weights = exponent.astype(jnp.bfloat16)
    values = jnp.concatenate([blocks[j, BLOCK : 2 * BLOCK] for j in range(PICKS)], axis=0)
    ones = jnp.ones((PICKS * BLOCK, HEAD_DIM), jnp.bfloat16)
    mixed = jnp.dot(
        weights, jnp.concatenate([values, ones], axis=1), preferred_element_type=jnp.float32
    )
    return (mixed[:, :HEAD_DIM] / mixed[:, HEAD_DIM:]).astype(jnp.bfloat16)


def attend(first, query_ref, member, bias_ref, blocks_ref, own_ref, far_ref):
    half, width = own_ref.shape
    count = width // HEAD_DIM
    blocks_of = lambda n: blocks_ref.at[n * PICKS : (n + 1) * PICKS]

    def score_of(n):
        cut = slice(n * HEAD_DIM, (n + 1) * HEAD_DIM)
        return score(first + n, query_ref[:, cut], member, bias_ref, blocks_of(n))

    following = score_of(0)
    for n in range(count):
        scores = following
        if n + 1 < count:
            following = score_of(n + 1)
        mixed = mix(scores, blocks_of(n))
        cut = slice(n * HEAD_DIM, (n + 1) * HEAD_DIM)
        own_ref[:, cut] = mixed[:half]
        far_ref[:, cut] = mixed[half:]


def first_kernel(
    position_ref, member_ref, bias_ref, query_own, query_far, got_ref,
    own_ref, far_ref, later_blocks, later_query, blocks, query, block_sem, query_sem,
):
    heads = position_ref.shape[0]
    half = own_ref.shape[0]
    count = own_ref.shape[1] // HEAD_DIM
    width = heads * HEAD_DIM
    base = lax.axis_index("head") * width

    def query_copies(first, target, n):
        cut = pl.ds(pl.multiple_of(base + first * HEAD_DIM, 128), target.shape[1])
        return [
            pltpu.make_async_copy(
                source.at[:, cut], target.at[r * half : (r + 1) * half], query_sem.at[n, r]
            )
            for r, source in enumerate((query_own, query_far))
        ]

    def block_copy(h, j):
        target = blocks.at[h * PICKS + j] if h < count else later_blocks.at[(h - count) * PICKS + j]
        return pltpu.make_async_copy(
            got_ref.at[position_ref[h, j]], target, block_sem.at[0 if h < count else 1]
        )

    now, later = query_copies(0, query, 0), query_copies(count, later_query, 1)
    for copy in now:
        copy.start()
    for h in range(count):
        for j in range(PICKS):
            block_copy(h, j).start()
    for copy in later:
        copy.start()
    for h in range(count, heads):
        for j in range(PICKS):
            block_copy(h, j).start()
    for copy in now:
        copy.wait()
    pltpu.make_async_copy(blocks, blocks, block_sem.at[0]).wait()
    attend(0, query, member_ref[...], bias_ref, blocks, own_ref, far_ref)
    for copy in later:
        copy.wait()
    pltpu.make_async_copy(later_blocks, later_blocks, block_sem.at[1]).wait()


def last_kernel(member_ref, bias_ref, blocks, query, own_ref, far_ref):
    first = bias_ref.shape[1] - own_ref.shape[1] // HEAD_DIM
    attend(first, query, member_ref[...], bias_ref, blocks, own_ref, far_ref)


def columns_of(out_ref, side, part_ref, first):
    start = side * (out_ref.shape[1] // 2) + first * HEAD_DIM
    return out_ref.at[:, pl.ds(pl.multiple_of(start, 128), part_ref.shape[1])]


def place_kernel(own_first, own_last, far_first, out_ref, sem):
    core = lax.axis_index("head")
    first = own_first.shape[1] // HEAD_DIM
    copies = [
        pltpu.make_async_copy(part, columns_of(out_ref, side, part, at), sem.at[n])
        for n, (part, side, at) in enumerate(
            ((own_first, core, 0), (own_last, core, first), (far_first, 1 - core, 0))
        )
    ]
    for copy in copies:
        copy.start()
    for copy in copies:
        copy.wait()


def place_last_kernel(out_in, far_last, out_ref, sem):
    del out_in
    first = (out_ref.shape[1] // 2 - far_last.shape[1]) // HEAD_DIM
    side = 1 - lax.axis_index("head")
    copy = pltpu.make_async_copy(far_last, columns_of(out_ref, side, far_last, first), sem)
    copy.start()
    copy.wait()


def shards(queries, key_states, value_states, cluster_perm, block_mask):
    heads, rows = cluster_perm.shape
    half, columns = queries.shape
    width = heads * HEAD_DIM
    shard_blocks = rows // BLOCK
    seq_count = lax.axis_size("seq")
    pairs = heads * shard_blocks
    slots = seq_count * CAPACITY
    vmem = pl.BlockSpec(memory_space=pltpu.VMEM)
    smem = pl.BlockSpec(memory_space=pltpu.SMEM)
    hbm = pl.BlockSpec(memory_space=pltpu.HBM)
    limit = lambda mib: pltpu.CompilerParams(vmem_limit_bytes=mib << 20)
    held = lambda x: pltpu.with_memory_space_constraint(x, pltpu.VMEM)
    far = lambda x: pltpu.with_memory_space_constraint(x, pltpu.HBM)
    held_out = lambda shape, dtype: pltpu.VMEM(shape, dtype)
    hbm_out = lambda shape, dtype: pltpu.HBM(shape, dtype)
    dma = pltpu.SemaphoreType.DMA
    bf16 = jnp.bfloat16

    table = pl.pallas_call(
        request_kernel,
        out_shape=jax.ShapeDtypeStruct((seq_count, 128), jnp.int32),
        in_specs=[vmem],
        out_specs=vmem,
        name="request",
    )(block_mask)
    requested = lax.all_to_all(
        table.reshape(seq_count, 1, 128), "seq", split_axis=0, concat_axis=0, tiled=True
    ).reshape(seq_count, 128)

    def swap(x):
        return lax.ppermute(x, "head", [(0, 1), (1, 0)])

    key_far = swap(key_states)
    value_far = swap(value_states)

    query_far = swap(queries)
    position, bias = pl.pallas_call(
        plan_kernel,
        out_shape=[
            jax.ShapeDtypeStruct((heads, 128), jnp.int32),
            jax.ShapeDtypeStruct((PICKS, heads, 128), jnp.float32),
        ],
        in_specs=[vmem],
        out_specs=[vmem] * 2,
        name="plan",
    )(block_mask)
    key_args = (far(key_states), key_far, far(value_states), value_far)

    def sort_scratch(count, step, kept):
        return [
            pltpu.VMEM((128, rows), jnp.float32),
            pltpu.VMEM((count // step, 4, half, step * HEAD_DIM), bf16),
            pltpu.VMEM((kept, 2 * BLOCK, HEAD_DIM), bf16),
            dma((count // step, 4)),
            dma,
            dma,
        ]

    early, early_member, column = pl.pallas_call(
        early_kernel,
        out_shape=[
            hbm_out((EARLY * shard_blocks, 2 * BLOCK, HEAD_DIM), bf16),
            jax.ShapeDtypeStruct((rows, 128), bf16),
            held_out((rows, 128), jnp.int32),
        ],
        in_specs=[hbm] * 5,
        out_specs=[hbm, vmem, vmem],
        scratch_shapes=[pltpu.VMEM((heads, rows), jnp.int32), pltpu.VMEM((128, rows), jnp.int32)]
        + sort_scratch(EARLY, EARLY, EARLY * shard_blocks),
        compiler_params=limit(24),
        name="early_sort",
    )(far(cluster_perm), *key_args)
    send, member = pl.pallas_call(
        sort_kernel,
        out_shape=[
            hbm_out((slots, 2 * BLOCK, HEAD_DIM), bf16),
            held_out((rows, 128), bf16),
        ],
        in_specs=[smem, vmem] + [hbm] * 5 + [vmem],
        out_specs=[hbm, vmem],
        scratch_shapes=sort_scratch(heads - EARLY, SORT_STEP, pairs),
        compiler_params=limit(32),
        name="sort",
    )(requested, held(column), *key_args, far(early), early_member)
    send, member, position, bias, query_far = lax.optimization_barrier(
        (send, member, position, bias, query_far)
    )
    got = lax.all_to_all(send, "seq", split_axis=0, concat_axis=0, tiled=True)

    first, last = heads - LAST, LAST
    part = lambda count: held_out((half, count * HEAD_DIM), bf16)
    own_first, far_first, later_blocks, later_query = pl.pallas_call(
        first_kernel,
        out_shape=[
            part(first),
            part(first),
            held_out((last * PICKS, 2 * BLOCK, HEAD_DIM), bf16),
            held_out((rows, last * HEAD_DIM), bf16),
        ],
        in_specs=[smem, vmem, vmem, hbm, hbm, hbm],
        out_specs=[vmem] * 4,
        scratch_shapes=[
            pltpu.VMEM((first * PICKS, 2 * BLOCK, HEAD_DIM), bf16),
            pltpu.VMEM((rows, first * HEAD_DIM), bf16),
            dma((2,)),
            dma((2, 2)),
        ],
        compiler_params=limit(24),
        name="first_heads",
    )(position, held(member), bias, far(queries), query_far, far(got))
    far_first = swap(far_first)
    own_last, far_last = pl.pallas_call(
        last_kernel,
        out_shape=[part(last), part(last)],
        in_specs=[vmem] * 4,
        out_specs=[vmem] * 2,
        compiler_params=limit(24),
        name="last_heads",
    )(held(member), bias, held(later_blocks), held(later_query))
    far_last = swap(far_last)
    out = pl.pallas_call(
        place_kernel,
        out_shape=hbm_out((half, columns), bf16),
        in_specs=[vmem] * 3,
        out_specs=hbm,
        scratch_shapes=[dma((3,))],
        compiler_params=limit(8),
        name="place",
    )(held(own_first), held(own_last), held(far_first))
    return pl.pallas_call(
        place_last_kernel,
        out_shape=hbm_out((half, columns), bf16),
        in_specs=[hbm, vmem],
        out_specs=hbm,
        scratch_shapes=[dma],
        input_output_aliases={0: 0},
        compiler_params=limit(8),
        name="place_last",
    )(out, held(far_last))


def solution(mesh):
    placed = (
        P(("seq", "head"), None),
        P(("seq", "head"), None),
        P(("seq", "head"), None),
        P("head", "seq"),
        P("head", "seq", None),
    )
    return jax.shard_map(
        shards, mesh=mesh, in_specs=placed, out_specs=P(("seq", "head"), None), check_vma=False
    )
```

```python
import math

import jax
import jax.numpy as jnp
from jax import lax
from jax.experimental import pallas as pl
from jax.experimental.pallas import tpu as pltpu
from jax.sharding import PartitionSpec as P

HEAD_DIM = 128
BLOCK = 128
CAPACITY = 2
PICKS = 4
EARLY = 10
SORT_STEP = 5
LAST = 6
MASKED = -1e30


def shift_of(count):
    return count.bit_length() - 1


def slot_lows(needed, shard_blocks):
    heads, blocks = needed.shape
    shards = blocks // shard_blocks
    key_block = lax.broadcasted_iota(jnp.int32, (heads, blocks), 1)
    head = lax.broadcasted_iota(jnp.int32, (heads, blocks), 0)
    pair = head * shard_blocks + jnp.bitwise_and(key_block, shard_blocks - 1)
    low = jnp.min(jnp.where(needed > 0, pair, heads * shard_blocks), axis=0, keepdims=True)
    owner = lax.broadcasted_iota(jnp.int32, (shards, blocks), 1) >> shift_of(shard_blocks)
    mine = owner == lax.broadcasted_iota(jnp.int32, (shards, blocks), 0)
    low_col = jnp.min(jnp.where(mine, low, heads * shard_blocks), axis=1, keepdims=True)
    return pair, mine, low_col


def request_kernel(mask_ref, table_ref):
    heads, shard_blocks, blocks = mask_ref.shape
    shards = blocks >> shift_of(shard_blocks)
    count = heads * shard_blocks
    mask = mask_ref[...]
    head = lax.broadcasted_iota(jnp.int32, mask.shape, 0)
    key_block = lax.broadcasted_iota(jnp.int32, mask.shape, 2)
    pair = head * shard_blocks + jnp.bitwise_and(key_block, shard_blocks - 1)
    low = jnp.min(jnp.where(mask > 0, pair, count), axis=0)
    high = jnp.max(jnp.where(mask > 0, pair, -1), axis=0)
    low = jnp.min(low, axis=0, keepdims=True)
    high = jnp.max(high, axis=0, keepdims=True)
    owner = lax.broadcasted_iota(jnp.int32, (shards, blocks), 1) >> shift_of(shard_blocks)
    mine = owner == lax.broadcasted_iota(jnp.int32, (shards, blocks), 0)
    low_col = jnp.min(jnp.where(mine, low, count), axis=1, keepdims=True)
    high_col = jnp.max(jnp.where(mine, high, -1), axis=1, keepdims=True)
    high_col = jnp.where(high_col == low_col, -1, high_col)
    low_col = jnp.where(low_col == count, -1, low_col)
    lane = lax.broadcasted_iota(jnp.int32, table_ref.shape, 1)
    table_ref[...] = jnp.where(lane == 0, low_col, high_col)


def local_tokens(perm, rows):
    return jnp.bitwise_and(perm + lax.axis_index("head") * (rows // 2), rows - 1)


def plan(mask_ref, position_ref, bias_ref):
    heads, shard_blocks, blocks = mask_ref.shape
    mask = mask_ref[...]
    needed = jnp.max(mask, axis=1)
    pair, mine, low_col = slot_lows(needed, shard_blocks)
    low_own = jnp.min(jnp.where(mine, low_col, heads * shard_blocks), axis=0, keepdims=True)
    key_block = lax.broadcasted_iota(jnp.int32, (heads, blocks), 1)
    slot = (key_block >> shift_of(shard_blocks)) * CAPACITY + (pair != low_own).astype(jnp.int32)
    upper = (
        lax.broadcasted_iota(jnp.int32, (blocks, blocks), 0)
        < lax.broadcasted_iota(jnp.int32, (blocks, blocks), 1)
    )
    prefix = jnp.dot(
        needed.astype(jnp.float32).astype(jnp.bfloat16),
        jnp.where(upper, 1.0, 0.0).astype(jnp.bfloat16),
        preferred_element_type=jnp.float32,
    )
    lane = lax.broadcasted_iota(jnp.int32, (heads, 128), 1)
    row = lax.broadcasted_iota(jnp.int32, (heads, 128), 0)
    position = jnp.zeros((heads, 128), jnp.int32)
    for j in range(PICKS):
        chosen = (needed > 0) & (prefix == float(j))
        slot_j = jnp.sum(jnp.where(chosen, slot, 0), axis=1, keepdims=True)
        position = jnp.where(lane == j, slot_j, position)
        bias = jnp.zeros((heads, 128), jnp.float32)
        for q in range(shard_blocks):
            live = jnp.max(jnp.where(chosen, mask[:, q, :], 0), axis=1, keepdims=True)
            bias = jnp.where((lane == row * shard_blocks + q) & (live == 0), MASKED, bias)
        bias_ref[j] = bias
    position_ref[...] = position


def sort_heads(first, heads, sources, column_of, out_ref, member_pad, buf, sem):
    steps, _, half, step_width = buf.shape
    rows = 2 * half
    step_heads = step_width // HEAD_DIM
    count = steps * step_heads
    shard_blocks = rows // BLOCK
    base = (lax.axis_index("head") * heads + first) * HEAD_DIM

    def copies(g):
        cut = pl.ds(pl.multiple_of(base + g * step_width, 128), step_width)
        return [
            pltpu.make_async_copy(ref.at[:, cut], buf.at[g, n], sem.at[g, n])
            for n, ref in enumerate(sources)
        ]

    for g in range(steps):
        for copy in copies(g):
            copy.start()
    member_pad[...] = jnp.zeros(member_pad.shape, jnp.float32)
    token = lax.broadcasted_iota(jnp.int32, (rows, half), 1)
    token = token.astype(jnp.float32).astype(jnp.bfloat16)
    column = column_of()
    own_column = jnp.where(column < half, column, -1).astype(jnp.float32)
    far_column = jnp.where(column < half, -1, column - half).astype(jnp.float32)

    def order_of(h):
        parts = []
        for table in (own_column, far_column):
            wide = jnp.broadcast_to(table[:, h : h + 1], (rows, 128)).astype(jnp.bfloat16)
            wide = jnp.tile(wide, (1, half // 128))
            parts.append(jnp.where(wide == token, jnp.bfloat16(1.0), jnp.bfloat16(0.0)))
        return jnp.concatenate(parts, axis=1)

    def block_sum(part):
        while part.shape[0] > 16:
            middle = part.shape[0] // 2
            part = part[:middle] + part[middle:]
        return jnp.sum(part.astype(jnp.float32), axis=0, keepdims=True)

    following = order_of(first)
    for n in range(count):
        order = following
        if n + 1 < count:
            following = order_of(first + n + 1)
        g, k = divmod(n, step_heads)
        if k == 0:
            for copy in copies(g):
                copy.wait()
        cut = slice(k * HEAD_DIM, (k + 1) * HEAD_DIM)
        own = jnp.concatenate([buf[g, 0, :, cut], buf[g, 1, :, cut]], axis=1)
        far = jnp.concatenate([buf[g, 2, :, cut], buf[g, 3, :, cut]], axis=1)
        ordered = jnp.dot(
            order, jnp.concatenate([own, far], axis=0), preferred_element_type=jnp.float32
        ).astype(jnp.bfloat16)
        for b in range(shard_blocks):
            part = slice(b * BLOCK, (b + 1) * BLOCK)
            row = (first + n) * shard_blocks + b
            member_pad[row : row + 1, :] = block_sum(order[part])
            slot = n * shard_blocks + b
            out_ref[slot, 0:BLOCK] = ordered[part, :HEAD_DIM]
            out_ref[slot, BLOCK : 2 * BLOCK] = ordered[part, HEAD_DIM:]
    return jnp.transpose(member_pad[...])


def early_kernel(
    mask_ref, perm_hbm, key_own, key_far, value_own, value_far,
    early_ref, member_ref, column_ref, position_ref, bias_ref, perm_raw, perm_pad, member_pad, buf, blocks,
    sem, perm_sem, out_sem,
):
    heads, rows = perm_hbm.shape
    perm_copy = pltpu.make_async_copy(perm_hbm, perm_raw, perm_sem)
    perm_copy.start()

    def column_of():
        plan(mask_ref, position_ref, bias_ref)
        perm_copy.wait()
        perm_pad[0:heads, :] = perm_raw[...]
        column = jnp.transpose(local_tokens(perm_pad[...], rows))
        column_ref[...] = column
        return column

    sources = (key_own, value_own, key_far, value_far)
    member = sort_heads(0, heads, sources, column_of, blocks, member_pad, buf, sem)
    copy = pltpu.make_async_copy(blocks, early_ref, out_sem)
    copy.start()
    member_ref[...] = member.astype(jnp.bfloat16)
    copy.wait()


def sort_kernel(
    request_ref, column_ref, key_own, key_far, value_own, value_far, early_ref, early_member,
    send_ref, member_ref, member_pad, buf, blocks, sem, early_sem, send_sem,
):
    early_count = early_ref.shape[0]
    heads = blocks.shape[0] * BLOCK // column_ref.shape[0]
    sources = (key_own, value_own, key_far, value_far)
    early_copy = pltpu.make_async_copy(early_ref, blocks.at[0:early_count], early_sem)

    def column_of():
        early_copy.start()
        return column_ref[...]

    member = sort_heads(
        EARLY, heads, sources, column_of, blocks.at[early_count:], member_pad, buf, sem
    )
    early_copy.wait()

    def start(d, count):
        for j in range(CAPACITY):
            asked = request_ref[d, j]

            @pl.when(asked >= 0)
            def _():
                pltpu.make_async_copy(
                    blocks.at[asked], send_ref.at[d * CAPACITY + j], send_sem
                ).start()

            count = count + (asked >= 0).astype(jnp.int32)
        return count

    started = lax.fori_loop(0, request_ref.shape[0], start, jnp.int32(0), unroll=8)
    member_ref[...] = (member + early_member[...].astype(jnp.float32)).astype(jnp.bfloat16)

    def finish(n, carry):
        pltpu.make_async_copy(blocks.at[0], send_ref.at[0], send_sem).wait()
        return carry

    lax.fori_loop(0, started, finish, 0)


def score(h, query, member, bias_ref, blocks):
    keys = []
    for j in range(PICKS):
        bias = jnp.broadcast_to(bias_ref[j, h : h + 1, :].astype(jnp.bfloat16), (BLOCK, 128))
        keys.append(jnp.concatenate([blocks[j, 0:BLOCK], bias], axis=1))
    return lax.dot_general(
        jnp.concatenate([query, member], axis=1),
        jnp.concatenate(keys, axis=0),
        (((1,), (1,)), ((), ())),
        preferred_element_type=jnp.float32,
    )


def mix(scores, blocks):
    top = jnp.max(scores, axis=1, keepdims=True)
    exponent = jnp.exp2((scores - top) * (math.log2(math.e) / math.sqrt(HEAD_DIM)))
    weights = exponent.astype(jnp.bfloat16)
    values = jnp.concatenate([blocks[j, BLOCK : 2 * BLOCK] for j in range(PICKS)], axis=0)
    ones = jnp.ones((PICKS * BLOCK, HEAD_DIM), jnp.bfloat16)
    mixed = jnp.dot(
        weights, jnp.concatenate([values, ones], axis=1), preferred_element_type=jnp.float32
    )
    return (mixed[:, :HEAD_DIM] / mixed[:, HEAD_DIM:]).astype(jnp.bfloat16)


def attend(first, query_ref, member, bias_ref, blocks_ref, own_ref, far_ref):
    half, width = own_ref.shape
    count = width // HEAD_DIM
    blocks_of = lambda n: blocks_ref.at[n * PICKS : (n + 1) * PICKS]

    def score_of(n):
        cut = slice(n * HEAD_DIM, (n + 1) * HEAD_DIM)
        return score(first + n, query_ref[:, cut], member, bias_ref, blocks_of(n))

    following = score_of(0)
    for n in range(count):
        scores = following
        if n + 1 < count:
            following = score_of(n + 1)
        mixed = mix(scores, blocks_of(n))
        cut = slice(n * HEAD_DIM, (n + 1) * HEAD_DIM)
        own_ref[:, cut] = mixed[:half]
        far_ref[:, cut] = mixed[half:]


def first_kernel(
    position_ref, member_ref, bias_ref, query_own, query_far, got_ref,
    own_ref, far_ref, later_blocks, later_query, blocks, query, block_sem, query_sem,
):
    heads = position_ref.shape[0]
    half = own_ref.shape[0]
    count = own_ref.shape[1] // HEAD_DIM
    width = heads * HEAD_DIM
    base = lax.axis_index("head") * width

    def query_copies(first, target, n):
        cut = pl.ds(pl.multiple_of(base + first * HEAD_DIM, 128), target.shape[1])
        return [
            pltpu.make_async_copy(
                source.at[:, cut], target.at[r * half : (r + 1) * half], query_sem.at[n, r]
            )
            for r, source in enumerate((query_own, query_far))
        ]

    def block_copy(h, j):
        target = blocks.at[h * PICKS + j] if h < count else later_blocks.at[(h - count) * PICKS + j]
        return pltpu.make_async_copy(
            got_ref.at[position_ref[h, j]], target, block_sem.at[0 if h < count else 1]
        )

    now, later = query_copies(0, query, 0), query_copies(count, later_query, 1)
    for copy in now:
        copy.start()
    for h in range(count):
        for j in range(PICKS):
            block_copy(h, j).start()
    for copy in later:
        copy.start()
    for h in range(count, heads):
        for j in range(PICKS):
            block_copy(h, j).start()
    for copy in now:
        copy.wait()
    pltpu.make_async_copy(blocks, blocks, block_sem.at[0]).wait()
    attend(0, query, member_ref[...], bias_ref, blocks, own_ref, far_ref)
    for copy in later:
        copy.wait()
    pltpu.make_async_copy(later_blocks, later_blocks, block_sem.at[1]).wait()


def last_kernel(member_ref, bias_ref, blocks, query, own_ref, far_ref):
    first = bias_ref.shape[1] - own_ref.shape[1] // HEAD_DIM
    attend(first, query, member_ref[...], bias_ref, blocks, own_ref, far_ref)


def columns_of(out_ref, side, part_ref, first):
    start = side * (out_ref.shape[1] // 2) + first * HEAD_DIM
    return out_ref.at[:, pl.ds(pl.multiple_of(start, 128), part_ref.shape[1])]


def place_kernel(own_first, own_last, far_first, out_ref, sem):
    core = lax.axis_index("head")
    first = own_first.shape[1] // HEAD_DIM
    copies = [
        pltpu.make_async_copy(part, columns_of(out_ref, side, part, at), sem.at[n])
        for n, (part, side, at) in enumerate(
            ((own_first, core, 0), (own_last, core, first), (far_first, 1 - core, 0))
        )
    ]
    for copy in copies:
        copy.start()
    for copy in copies:
        copy.wait()


def place_last_kernel(out_in, far_last, out_ref, sem):
    del out_in
    first = (out_ref.shape[1] // 2 - far_last.shape[1]) // HEAD_DIM
    side = 1 - lax.axis_index("head")
    copy = pltpu.make_async_copy(far_last, columns_of(out_ref, side, far_last, first), sem)
    copy.start()
    copy.wait()


def shards(queries, key_states, value_states, cluster_perm, block_mask):
    heads, rows = cluster_perm.shape
    half, columns = queries.shape
    width = heads * HEAD_DIM
    shard_blocks = rows // BLOCK
    seq_count = lax.axis_size("seq")
    pairs = heads * shard_blocks
    slots = seq_count * CAPACITY
    vmem = pl.BlockSpec(memory_space=pltpu.VMEM)
    smem = pl.BlockSpec(memory_space=pltpu.SMEM)
    hbm = pl.BlockSpec(memory_space=pltpu.HBM)
    limit = lambda mib: pltpu.CompilerParams(vmem_limit_bytes=mib << 20)
    held = lambda x: pltpu.with_memory_space_constraint(x, pltpu.VMEM)
    far = lambda x: pltpu.with_memory_space_constraint(x, pltpu.HBM)
    held_out = lambda shape, dtype: pltpu.VMEM(shape, dtype)
    hbm_out = lambda shape, dtype: pltpu.HBM(shape, dtype)
    dma = pltpu.SemaphoreType.DMA
    bf16 = jnp.bfloat16

    table = pl.pallas_call(
        request_kernel,
        out_shape=jax.ShapeDtypeStruct((seq_count, 128), jnp.int32),
        in_specs=[vmem],
        out_specs=vmem,
        name="request",
    )(block_mask)
    requested = lax.all_to_all(
        table.reshape(seq_count, 1, 128), "seq", split_axis=0, concat_axis=0, tiled=True
    ).reshape(seq_count, 128)

    def swap(x):
        return lax.ppermute(x, "head", [(0, 1), (1, 0)])

    key_far = swap(key_states)
    value_far = swap(value_states)

    query_far = swap(queries)
    key_args = (far(key_states), key_far, far(value_states), value_far)

    def sort_scratch(count, step, kept):
        return [
            pltpu.VMEM((128, rows), jnp.float32),
            pltpu.VMEM((count // step, 4, half, step * HEAD_DIM), bf16),
            pltpu.VMEM((kept, 2 * BLOCK, HEAD_DIM), bf16),
            dma((count // step, 4)),
            dma,
            dma,
        ]

    early, early_member, column, position, bias = pl.pallas_call(
        early_kernel,
        out_shape=[
            hbm_out((EARLY * shard_blocks, 2 * BLOCK, HEAD_DIM), bf16),
            jax.ShapeDtypeStruct((rows, 128), bf16),
            held_out((rows, 128), jnp.int32),
            jax.ShapeDtypeStruct((heads, 128), jnp.int32),
            jax.ShapeDtypeStruct((PICKS, heads, 128), jnp.float32),
        ],
        in_specs=[vmem] + [hbm] * 5,
        out_specs=[hbm] + [vmem] * 4,
        scratch_shapes=[pltpu.VMEM((heads, rows), jnp.int32), pltpu.VMEM((128, rows), jnp.int32)]
        + sort_scratch(EARLY, EARLY, EARLY * shard_blocks),
        compiler_params=limit(24),
        name="early_sort",
    )(block_mask, far(cluster_perm), *key_args)
    send, member = pl.pallas_call(
        sort_kernel,
        out_shape=[
            hbm_out((slots, 2 * BLOCK, HEAD_DIM), bf16),
            held_out((rows, 128), bf16),
        ],
        in_specs=[smem, vmem] + [hbm] * 5 + [vmem],
        out_specs=[hbm, vmem],
        scratch_shapes=sort_scratch(heads - EARLY, SORT_STEP, pairs),
        compiler_params=limit(32),
        name="sort",
    )(requested, held(column), *key_args, far(early), early_member)
    send, member, position, bias, query_far = lax.optimization_barrier(
        (send, member, position, bias, query_far)
    )
    got = lax.all_to_all(send, "seq", split_axis=0, concat_axis=0, tiled=True)

    first, last = heads - LAST, LAST
    part = lambda count: held_out((half, count * HEAD_DIM), bf16)
    own_first, far_first, later_blocks, later_query = pl.pallas_call(
        first_kernel,
        out_shape=[
            part(first),
            part(first),
            held_out((last * PICKS, 2 * BLOCK, HEAD_DIM), bf16),
            held_out((rows, last * HEAD_DIM), bf16),
        ],
        in_specs=[smem, vmem, vmem, hbm, hbm, hbm],
        out_specs=[vmem] * 4,
        scratch_shapes=[
            pltpu.VMEM((first * PICKS, 2 * BLOCK, HEAD_DIM), bf16),
            pltpu.VMEM((rows, first * HEAD_DIM), bf16),
            dma((2,)),
            dma((2, 2)),
        ],
        compiler_params=limit(24),
        name="first_heads",
    )(position, held(member), bias, far(queries), query_far, far(got))
    far_first = swap(far_first)
    own_last, far_last = pl.pallas_call(
        last_kernel,
        out_shape=[part(last), part(last)],
        in_specs=[vmem] * 4,
        out_specs=[vmem] * 2,
        compiler_params=limit(24),
        name="last_heads",
    )(held(member), bias, held(later_blocks), held(later_query))
    far_last = swap(far_last)
    out = pl.pallas_call(
        place_kernel,
        out_shape=hbm_out((half, columns), bf16),
        in_specs=[vmem] * 3,
        out_specs=hbm,
        scratch_shapes=[dma((3,))],
        compiler_params=limit(8),
        name="place",
    )(held(own_first), held(own_last), held(far_first))
    return pl.pallas_call(
        place_last_kernel,
        out_shape=hbm_out((half, columns), bf16),
        in_specs=[hbm, vmem],
        out_specs=hbm,
        scratch_shapes=[dma],
        input_output_aliases={0: 0},
        compiler_params=limit(8),
        name="place_last",
    )(out, held(far_last))


def solution(mesh):
    placed = (
        P(("seq", "head"), None),
        P(("seq", "head"), None),
        P(("seq", "head"), None),
        P("head", "seq"),
        P("head", "seq", None),
    )
    return jax.shard_map(
        shards, mesh=mesh, in_specs=placed, out_specs=P(("seq", "head"), None), check_vma=False
    )
```
